32 devices in a mesh: groups: 2 (over y), shard: 16 (over z, x, core).
Axes of the slice: x: 2, y: 2, z: 4, core: 2. Of those that a mesh axis runs over, the one named last changes fastest.
Arguments:
- traces: float32 [20736, 2048], P(('groups', 'shard')), parts along dimension 0, may hold values from -250 to 250
- cable_depth: float32 [32], P(('groups', 'shard')), parts along dimension 0, may hold values from 6 to 25
- receiver: int32 [20736], P(('groups', 'shard')), parts along dimension 0, may hold values from 0 to 671, as said below
- shot_slot: int32 [32], P('groups'), parts along dimension 0, may hold values from 0 to 15, as said below
- gather_home: int32 [1344], P('groups'), parts along dimension 0, may hold values from 0 to 671, each once
Outputs:
- filtered_gathers: float32 [1344, 16, 2048], P(('groups', 'shard')), parts along dimension 0
The draws below stay inside these ranges and needn't reach their ends.
There are 2 independent parts, one for each index of `groups`. The reference program is written for one: setup_inputs(seed, part) draws one part's arguments, and reference() takes and returns one part's arrays. A program takes and returns all parts, laid end to end along the dimension named above; each array names one. Nothing has to cross between parts.
Inputs may be any that keep to these rules, and one draw needn't show every extreme that they name: The 648 receiver bins of one record are distinct. `shot_slot`: every record has a position of its own.
All inputs are finite; a program needn't handle non-finite values.
Results may differ from the reference program's by a relative error of at most 0.0081.
Values may be sent and summed in bfloat16 or wider, within the bound.
No kernel may reach another device: no remote copies, remote signals or barrier semaphores. Data moves between devices by JAX's collectives and lax.ppermute only.
A program may use at most 64 MiB of HBM per device.

```python
import math
import jax
import jax.numpy as jnp
from jax import lax

NT = 2048
NCH = 648
FREQ = 576
RECORDS = 16
TRACES = 10368
NREC = 672


def slot_order(key):
    return jax.random.permutation(jax.random.fold_in(key, 17), RECORDS).astype(jnp.int32)


def draw_shot_slot(key, part):
    return slot_order(key)


def draw_receiver(key, part):
    slots = slot_order(key)
    room = NREC - NCH - RECORDS + 1
    skips = jax.random.randint(jax.random.fold_in(key, 23), (RECORDS, NCH), 0, 2).astype(jnp.int32)
    skipped = jnp.cumsum(skips, axis=1) - skips
    channels = jnp.arange(NCH, dtype=jnp.int32)
    bins = slots[:, None] + channels[None, :] + jnp.minimum(skipped, room)
    bins = jnp.where(channels[None, :] == NCH - 1, slots[:, None] + NCH - 1 + room, bins)
    return bins.reshape(TRACES).astype(jnp.int32)


def draw_traces(key, part):
    record_index = (jnp.arange(TRACES, dtype=jnp.int32) // NCH).astype(jnp.float32)
    ramp = jnp.exp(0.5 * math.log(3.0) * record_index / max(RECORDS - 1, 1))
    sample_index = jnp.arange(NT, dtype=jnp.float32) / NT
    noise = jnp.clip(jax.random.normal(jax.random.fold_in(key, 31), (TRACES, NT), jnp.float32), -6.0, 6.0)
    decay = jnp.exp(-math.log(10.0) * sample_index)
    trace_scale = jnp.exp(jax.random.uniform(jax.random.fold_in(key, 41), (TRACES,), jnp.float32, 0.0, math.log(10.0)))
    return (noise * (ramp * trace_scale)[:, None] * decay[None, :]).astype(jnp.float32)


def block_scale(rng, extent, cuts, smallest, largest):
    def one(dim, blocks):
        heights = jax.random.uniform(jax.random.fold_in(jax.random.fold_in(rng, 6), dim), (blocks,), jnp.float32, smallest / len(cuts), largest / len(cuts))
        return jnp.repeat(jnp.exp(heights), extent[dim] // blocks).reshape((-1,) + (1,) * (len(extent) - dim - 1))

    factor_of = one(*cuts[0])
    for cut in cuts[1:]:
        factor_of = factor_of * one(*cut)
    return factor_of


def setup_inputs(seed: int = 0, part: int = 0) -> dict:
    streams_of = jax.random.split(jax.random.key(seed), 6)
    part_keys = jax.random.split(jax.random.fold_in(streams_of[5], part), 6)
    return {
        "traces": draw_traces(jax.random.fold_in(jax.random.fold_in(streams_of[5], part), 71), part),
        "cable_depth": jnp.clip(6.0 + 19.0 * jax.random.uniform(part_keys[1], (RECORDS,), jnp.float32) ** block_scale(part_keys[1], (RECORDS,), ((0, 16),), -0.2, 0.2), 6.0, 25.0),
        "receiver": draw_receiver(jax.random.fold_in(jax.random.fold_in(streams_of[5], part), 71), part),
        "shot_slot": draw_shot_slot(jax.random.fold_in(jax.random.fold_in(streams_of[5], part), 71), part),
        "gather_home": jax.random.permutation(part_keys[4], NREC).astype(jnp.int32),
    }


sample_step = 0.002
water_speed = 1500.0
channel_spacing = 12.5
shot_spacing = 25.0
surface_reflect = 0.9
ghost_floor = 0.1
reject_speed = 1500.0
low_floor = 4.0 * math.pi
energy_eps = 1e-06

def forward_time(n_samples, first_bin, band_size):
    samples = jnp.arange(n_samples, dtype=jnp.int32)
    freq_bins = first_bin + jnp.arange(band_size, dtype=jnp.int32)
    angles = (samples[:, None] * freq_bins[None, :] % n_samples).astype(jnp.float32) * (2.0 * math.pi / n_samples)
    return jnp.concatenate([jnp.cos(angles), -jnp.sin(angles)], axis=1).astype(jnp.bfloat16)

def inverse_time(n_samples, first_bin, band_size):
    samples = jnp.arange(n_samples, dtype=jnp.int32)
    freq_bins = first_bin + jnp.arange(band_size, dtype=jnp.int32)
    angles = (freq_bins[:, None] * samples[None, :] % n_samples).astype(jnp.float32) * (2.0 * math.pi / n_samples)
    weights = jnp.where(freq_bins == 0, 1.0, 2.0).astype(jnp.float32)[:, None]
    return jnp.concatenate([weights * jnp.cos(angles), -weights * jnp.sin(angles)], axis=0).astype(jnp.bfloat16)

def wave_tables(n_channels):
    wave_index = jnp.arange(n_channels, dtype=jnp.int32)
    angles = (wave_index[:, None] * wave_index[None, :] % n_channels).astype(jnp.float32) * (2.0 * math.pi / n_channels)
    return (jnp.cos(angles).astype(jnp.bfloat16), jnp.sin(angles).astype(jnp.bfloat16))

def angular_band(n_samples, first_bin, band_size):
    freq_bins = (first_bin + jnp.arange(band_size, dtype=jnp.int32)).astype(jnp.float32)
    return 2.0 * math.pi * freq_bins / (n_samples * sample_step)

def ghost_operator(n_channels, n_samples, first_bin, band_size, depth_value):
    angular = angular_band(n_samples, first_bin, band_size)
    wave_index = jnp.arange(n_channels, dtype=jnp.int32)
    signed = jnp.where(wave_index <= n_channels // 2, wave_index, wave_index - n_channels).astype(jnp.float32)
    wave_number = 2.0 * math.pi * signed / (n_channels * channel_spacing)
    slowness = angular / water_speed
    vertical = jnp.sqrt(jnp.maximum(slowness[None, :] * slowness[None, :] - wave_number[:, None] * wave_number[:, None], 0.0))
    angles = 2.0 * vertical * depth_value
    cosine = jnp.cos(angles)
    denominator = 1.0 - 2.0 * surface_reflect * cosine + surface_reflect * surface_reflect + ghost_floor
    return ((1.0 - surface_reflect * cosine) / denominator, -surface_reflect * jnp.sin(angles) / denominator)

def deghost(record, depth_value, first_bin, band_size):
    n_channels, n_samples = record.shape
    spectra = jnp.dot(record.astype(jnp.bfloat16), forward_time(n_samples, first_bin, band_size), preferred_element_type=jnp.float32).astype(jnp.bfloat16)
    cos_wave, sin_wave = wave_tables(n_channels)
    plain = jnp.dot(cos_wave, spectra, preferred_element_type=jnp.float32)
    turned = jnp.dot(sin_wave, spectra, preferred_element_type=jnp.float32)
    wave_re = plain[:, :band_size] + turned[:, band_size:]
    wave_im = plain[:, band_size:] - turned[:, :band_size]
    gain_re, gain_im = ghost_operator(n_channels, n_samples, first_bin, band_size, depth_value)
    lifted = jnp.concatenate([gain_re * wave_re - gain_im * wave_im, gain_re * wave_im + gain_im * wave_re], axis=1).astype(jnp.bfloat16)
    plain = jnp.dot(cos_wave, lifted, preferred_element_type=jnp.float32)
    turned = jnp.dot(sin_wave, lifted, preferred_element_type=jnp.float32)
    back_re = (plain[:, :band_size] - turned[:, band_size:]) / n_channels
    back_im = (plain[:, band_size:] + turned[:, :band_size]) / n_channels
    cleaned = jnp.concatenate([back_re, back_im], axis=1)
    return (cleaned.astype(jnp.bfloat16), jnp.sum(cleaned * cleaned))

def shot_tables(positions, records):
    wave_index = jnp.arange(2 * records, dtype=jnp.int32)
    angles = (positions[:, None] * wave_index[None, :] % (2 * records)).astype(jnp.float32) * (math.pi / records)
    return (jnp.cos(angles).astype(jnp.bfloat16), jnp.sin(angles).astype(jnp.bfloat16))

def shot_filter(records, n_samples, first_bin, band_size):
    angular = angular_band(n_samples, first_bin, band_size)
    wave_index = jnp.arange(2 * records, dtype=jnp.int32)
    signed = jnp.where(wave_index <= records, wave_index, wave_index - 2 * records).astype(jnp.float32)
    shot_number = 2.0 * math.pi * signed / (2 * records * shot_spacing)
    reject_ratio = reject_speed * jnp.abs(shot_number)[:, None] / (angular[None, :] + low_floor)
    squared = reject_ratio * reject_ratio
    response = 1.0 / (1.0 + squared * squared) / (2.0 * records)
    return jnp.concatenate([response, response], axis=1)

def reference(traces, cable_depth, receiver, shot_slot, gather_home):
    records = cable_depth.shape[0]
    n_samples = traces.shape[1]
    stacked = traces.reshape(records, NCH, n_samples)

    def clean_one(item):
        record, depth_value = item
        return deghost(record, depth_value, 0, FREQ)
    clean_rows, energies = lax.map(clean_one, (stacked, cable_depth))
    total_energy = jnp.sum(energies)
    out_scale = 1.0 / jnp.sqrt(2.0 * FREQ * (total_energy / (TRACES * FREQ) + energy_eps))
    targets = jnp.take(gather_home, receiver, axis=0).astype(jnp.int32)
    positions = jnp.repeat(shot_slot, NCH).astype(jnp.int32)
    gathered = jnp.zeros((NREC, records, 2 * FREQ), jnp.bfloat16).at[targets, positions].set(clean_rows.reshape(TRACES, 2 * FREQ))
    cos_shot, sin_shot = shot_tables(jnp.arange(records, dtype=jnp.int32), records)
    response = shot_filter(records, n_samples, 0, FREQ)
    inverse = inverse_time(n_samples, 0, FREQ)

    def filter_one(gather):
        even_part = (jnp.dot(cos_shot.T, gather, preferred_element_type=jnp.float32) * response).astype(jnp.bfloat16)
        odd_part = (jnp.dot(sin_shot.T, gather, preferred_element_type=jnp.float32) * response).astype(jnp.bfloat16)
        filtered = (jnp.dot(cos_shot, even_part, preferred_element_type=jnp.float32) + jnp.dot(sin_shot, odd_part, preferred_element_type=jnp.float32)).astype(jnp.bfloat16)
        return jnp.dot(filtered, inverse, preferred_element_type=jnp.float32) * out_scale
    return lax.map(filter_one, gathered)
```

```python
import math

import jax
import jax.numpy as jnp
import ml_dtypes
import numpy as np
from jax import lax
from jax.experimental import pallas as pl
from jax.experimental.pallas import tpu as pltpu
from jax.sharding import PartitionSpec as P

FREQ = 576

sample_step = 0.002
water_speed = 1500.0
channel_spacing = 12.5
shot_spacing = 25.0
surface_reflect = 0.9
ghost_floor = 0.1
reject_speed = 1500.0
low_floor = 4.0 * math.pi
energy_eps = 1e-06

BF = jnp.bfloat16
F32 = jnp.float32
LANES = 128
HALF = 64


def to_bf16(table):
    return np.asarray(table, np.float32).astype(ml_dtypes.bfloat16)


def bin_tiles():
    even = np.arange(0, FREQ, 2)
    odd = np.arange(1, FREQ, 2)
    whole = len(even) // HALF
    left = len(even) - whole * HALF
    assert 2 * left == HALF and len(odd) == len(even)
    even_tiles = [even[j * HALF : (j + 1) * HALF] for j in range(whole)]
    odd_tiles = [odd[left + j * HALF : left + (j + 1) * HALF] for j in range(whole)]
    mixed = np.concatenate([even[whole * HALF :], odd[:left]])
    return even_tiles, odd_tiles, mixed


def time_table(n_samples, tiles, parity):
    samples = np.arange(n_samples // 2, dtype=np.int64)
    parts = []
    for bins in tiles:
        angle = (samples[:, None] * bins[None, :] % n_samples) * (2.0 * np.pi / n_samples)
        keep = (bins % 2 == parity).astype(np.float64)[None, :]
        parts += [np.cos(angle) * keep, -np.sin(angle) * keep]
    return to_bf16(np.concatenate(parts, axis=1))


def wave_rows(n_channels):
    return -(-(n_channels // 2 + 1) // 16) * 16


def wave_table(n_channels):
    rows = wave_rows(n_channels)
    k = np.arange(rows, dtype=np.int64)
    c = np.arange(n_channels, dtype=np.int64)
    angle = (k[:, None] * c[None, :] % n_channels) * (2.0 * np.pi / n_channels)
    live = (k <= n_channels // 2)[:, None]
    inner = ((k > 0) & (2 * k < n_channels))[:, None]
    return to_bf16(np.concatenate([np.cos(angle) * live, np.sin(angle) * inner], axis=0))


def vertical_table(n_channels, n_samples, tiles):
    rows = wave_rows(n_channels)
    k = np.minimum(np.arange(rows), n_channels // 2).astype(np.float64)
    kx = 2.0 * np.pi * k / (n_channels * channel_spacing)
    bins = np.concatenate(tiles).astype(np.float64)
    slow = 2.0 * np.pi * bins / (n_samples * sample_step) / water_speed
    return (2.0 * np.sqrt(np.maximum(slow[None, :] ** 2 - kx[:, None] ** 2, 0.0))).astype(np.float32)


def wave_weight(n_channels):
    rows = wave_rows(n_channels)
    k = np.arange(rows)
    single = (k == 0) | (2 * k == n_channels)
    weight = np.where(single, 1.0, 2.0) / n_channels
    return np.repeat(weight[:, None], LANES, axis=1).astype(np.float32)


def shot_basis(records):
    k = np.concatenate([np.arange(records + 1), np.arange(1, records)])
    p = np.arange(records)
    angle = (k[:, None] * p[None, :] % (2 * records)) * (np.pi / records)
    is_sin = (np.arange(2 * records) > records)[:, None]
    return np.where(is_sin, np.sin(angle), np.cos(angle)), k


def shot_forward(records, block):
    basis, _ = shot_basis(records)
    full = np.einsum("kp,gh->gkph", basis, np.eye(block))
    return to_bf16(full.reshape(block * 2 * records, records * block))


def shot_inverse(records, block):
    basis, _ = shot_basis(records)
    full = np.einsum("kp,gh->gphk", basis, np.eye(block))
    return to_bf16(full.reshape(block * records, block * 2 * records))


def response_table(records, n_samples, tiles):
    _, k = shot_basis(records)
    single = (k == 0) | (k == records)
    parts = []
    for bins in tiles:
        angular = 2.0 * np.pi * bins.astype(np.float64) / (n_samples * sample_step)
        shot_number = 2.0 * np.pi * k / (2 * records * shot_spacing)
        ratio = reject_speed * shot_number[:, None] / (angular[None, :] + low_floor)
        value = 1.0 / (1.0 + ratio**4) / (2.0 * records)
        value = value * np.where(single, 1.0, 2.0)[:, None] * np.where(bins == 0, 1.0, 2.0)[None, :]
        parts += [value, value]
    return np.concatenate(parts, axis=1).astype(np.float32)


def sin_cos(angle):
    turns = jnp.floor(angle * (2.0 / math.pi) + 0.5)
    rest = ((angle - turns * 1.5703125) - turns * 4.837512969970703125e-4) - turns * 7.54978995489188216e-8
    sq = rest * rest
    sine = ((-1.9515295891e-4 * sq + 8.3321608736e-3) * sq - 1.6666654611e-1) * sq * rest + rest
    cosine = ((2.443315711809948e-5 * sq - 1.388731625493765e-3) * sq + 4.166664568298827e-2) * sq * sq - 0.5 * sq + 1.0
    quarter = turns.astype(jnp.int32)
    odd = (quarter & 1) == 1
    sin_out = jnp.where(odd, cosine, sine)
    cos_out = jnp.where(odd, sine, cosine)
    sin_out = jnp.where((quarter & 2) == 2, -sin_out, sin_out)
    cos_out = jnp.where(((quarter + 1) & 2) == 2, -cos_out, cos_out)
    return sin_out, cos_out


def gains(vertical, depth, weight):
    sine, cosine = sin_cos(vertical * depth)
    denominator = 1.0 - 2.0 * surface_reflect * cosine + surface_reflect * surface_reflect + ghost_floor
    scale = weight / denominator
    return (1.0 - surface_reflect * cosine) * scale, -surface_reflect * sine * scale


def tile_gains(gain_re, gain_im, second):
    lane = lax.broadcasted_iota(jnp.int32, gain_re.shape, 1)
    low = lane < HALF
    re_other = pltpu.roll(gain_re, HALF, 1)
    im_other = pltpu.roll(gain_im, HALF, 1)
    if second:
        return jnp.where(low, re_other, gain_re), jnp.where(low, -im_other, gain_im)
    return jnp.where(low, gain_re, re_other), jnp.where(low, -gain_im, im_other)


def dot(a, b):
    return jnp.dot(a, b, preferred_element_type=F32)


def lift_and_place(spec_pair, n_tiles, vertical, depth, weight, wave_ref, place_ref, rows):
    plain = dot(wave_ref[...], spec_pair)
    gain_re, gain_im = gains(vertical, depth, weight)
    lifted = []
    for t in range(n_tiles):
        same, swapped = tile_gains(gain_re, gain_im, t == 1)
        both = []
        for h in range(2):
            part = plain[h * rows : (h + 1) * rows, t * LANES : (t + 1) * LANES]
            both.append((part * same + pltpu.roll(part, HALF, 1) * swapped).astype(BF))
        lifted.append(jnp.concatenate(both, axis=0))
    lifted = lifted[0] if n_tiles == 1 else jnp.concatenate(lifted, axis=1)
    return dot(place_ref[...], lifted)


def energy_of(placed):
    total = jnp.sum(placed * placed, axis=0, keepdims=True)
    return sum(total[:, t * LANES : (t + 1) * LANES] for t in range(placed.shape[1] // LANES))


def store_message(message_ref, placed, first_tile, blocks, block):
    n_dest = message_ref.shape[0]
    for t in range(placed.shape[1] // LANES):
        tile = placed[:, t * LANES : (t + 1) * LANES].astype(BF)
        j = first_tile + t
        message_ref[:, j * blocks : (j + 1) * blocks, :, :] = tile.reshape(n_dest, blocks, block, LANES)


def front_kernel(per, blocks, block, n_whole):
    def kernel(depth_ref, receiver_ref, home_ref, vertical_ref, weight_ref, traces_hbm, table_hbm, wave_ref, wave_t_ref,
               message_ref, odd_ref, mixed_ref, place_ref, energy_ref, traces_ref, table_ref, spec_ref, sems):
        n_channels, n_samples = traces_ref.shape
        half = n_samples // 2
        steps = 3
        step = n_channels // steps
        copies = []
        for s in range(steps):
            part = pl.ds(s * step, step)
            copies.append(pltpu.make_async_copy(traces_hbm.at[part, :], traces_ref.at[part, :], sems.at[s]))
        table_copy = pltpu.make_async_copy(table_hbm, table_ref, sems.at[steps])
        copies[0].start()
        table_copy.start()
        for c in copies[1:]:
            c.start()
        rows = wave_ref.shape[0] // 2
        n_rec = home_ref.shape[1]
        padded = blocks * block
        n_dest = message_ref.shape[0]
        home = home_ref[...].astype(F32)
        device = jnp.floor((home + 0.5) * (1.0 / per))
        home_row = (home + device * (padded - per)).astype(jnp.int32)
        to_home = lax.broadcasted_iota(jnp.int32, (n_dest * padded, n_rec), 0) == home_row
        to_home = jnp.where(to_home, 1.0, 0.0).astype(BF)
        to_bin = lax.broadcasted_iota(jnp.int32, (n_rec, n_channels), 0) == receiver_ref[...]
        to_bin = jnp.where(to_bin, 1.0, 0.0).astype(BF)
        picked = dot(to_home, to_bin).astype(BF)
        place_ref[...] = dot(picked, wave_t_ref[...]).astype(BF)
        table_copy.wait()
        for s in range(steps):
            copies[s].wait()
            part = pl.ds(s * step, step)
            first = traces_ref[part, :half]
            second = traces_ref[part, half:]
            odd_ref[part, :] = (first - second).astype(BF)
            got = dot((first + second).astype(BF), table_ref[...])
            spec_ref[part, :] = got[:, : n_whole * LANES].astype(BF)
            mixed_ref[part, :] = got[:, n_whole * LANES :]
        energy = jnp.zeros((1, LANES), F32)
        for pair in range(n_whole // 2):
            cols = slice(2 * pair * LANES, (2 * pair + 2) * LANES)
            placed = lift_and_place(spec_ref[:, cols], 2, vertical_ref[:, pair * LANES : (pair + 1) * LANES], depth_ref[0],
                                    weight_ref[...], wave_ref, place_ref, rows)
            energy = energy + energy_of(placed)
            store_message(message_ref, placed, 2 * pair, blocks, block)
        energy_ref[...] = energy

    return kernel


def second_kernel(blocks, block, n_whole):
    def kernel(depth_ref, vertical_ref, weight_ref, odd_ref, mixed_ref, place_ref, energy_ref, table_ref, wave_ref,
               message_ref, spec_ref):
        n_channels = odd_ref.shape[0]
        rows = wave_ref.shape[0] // 2
        got = dot(odd_ref[...], table_ref[...])
        whole = n_whole * LANES
        spec_ref[:, :whole] = got[:, :whole].astype(BF)
        spec_ref[:, whole:] = (got[:, whole:] + mixed_ref[...]).astype(BF)
        energy = energy_ref[...]
        for pair in range(n_whole // 2 + 1):
            n_tiles = 2 if pair < n_whole // 2 else 1
            cols = slice(2 * pair * LANES, (2 * pair + n_tiles) * LANES)
            placed = lift_and_place(spec_ref[:, cols], n_tiles, vertical_ref[:, pair * LANES : (pair + 1) * LANES], depth_ref[0],
                                    weight_ref[...], wave_ref, place_ref, rows)
            energy = energy + energy_of(placed)
            store_message(message_ref, placed, 2 * pair, blocks, block)
        total = jnp.sum(energy, axis=1, keepdims=True)
        high = total.astype(BF).astype(F32)
        middle = (total - high).astype(BF).astype(F32)
        low = total - high - middle
        lane = lax.broadcasted_iota(jnp.int32, (block, LANES), 1)
        row = lax.broadcasted_iota(jnp.int32, (block, LANES), 0)
        pieces = jnp.where(lane == 0, high, jnp.where(lane == 1, middle, jnp.where(lane == 2, low, 0.0)))
        n_dest = message_ref.shape[0]
        last = row == block - 1
        for d in range(n_dest):
            old = message_ref[d, blocks - 1].astype(F32)
            message_ref[d, blocks - 1] = jnp.where(last, pieces, old).astype(BF)

    return kernel


def arrive(slot_ref, arrived_hbm, x_ref, sems, block):
    copies = []
    for s in range(arrived_hbm.shape[0]):
        at = pl.multiple_of(slot_ref[s] * block, block)
        copies.append(pltpu.make_async_copy(arrived_hbm.at[s], x_ref.at[:, pl.ds(at, block), :], sems.at[s]))
    for c in copies:
        c.start()
    for c in copies:
        c.wait()


def filter_block(x_ref, forward_ref, inverse_ref, response_ref, b, blocks, tiles, block):
    out = []
    k = response_ref.shape[0]
    for first in range(0, tiles, 2):
        n = min(2, tiles - first)
        x = [x_ref[(first + t) * blocks + b] for t in range(n)]
        x = x[0] if n == 1 else jnp.concatenate(x, axis=1)
        part = dot(forward_ref[...], x).reshape(block, k, n * LANES)
        part = part * response_ref[:, first * LANES : (first + n) * LANES][None]
        part = part.reshape(block * k, n * LANES).astype(BF)
        out.append(dot(inverse_ref[...], part).astype(BF))
    return out[0] if len(out) == 1 else jnp.concatenate(out, axis=1)


def even_kernel(blocks, block, tiles):
    def kernel(slot_ref, arrived_hbm, forward_ref, inverse_ref, response_ref, table_ref, out_ref, x_ref, sems):
        arrive(slot_ref, arrived_hbm, x_ref, sems, block)
        size = inverse_ref.shape[0]
        for b in range(blocks):
            filtered = filter_block(x_ref, forward_ref, inverse_ref, response_ref, b, blocks, tiles, block)
            out_ref[pl.ds(b * size, size), :] = dot(filtered, table_ref[...])

    return kernel


def last_kernel(blocks, block, tiles, n_traces):
    def kernel(slot_ref, arrived_hbm, forward_ref, inverse_ref, response_ref, even_table_ref, odd_table_ref, even_ref,
               out_hbm, x_ref, out_ref, sems):
        arrive(slot_ref, arrived_hbm, x_ref, sems, block)
        records = arrived_hbm.shape[0]
        ends = x_ref[blocks - 1].astype(F32).reshape(records, block, LANES)
        row = lax.broadcasted_iota(jnp.int32, ends.shape, 1)
        lane = lax.broadcasted_iota(jnp.int32, ends.shape, 2)
        ends = jnp.where((row == block - 1) & (lane < 3), ends, 0.0)
        energy = jnp.sum(jnp.sum(ends, axis=0), keepdims=True)
        scale = lax.rsqrt(2.0 * FREQ * (energy * (1.0 / (n_traces * FREQ)) + energy_eps))
        size = inverse_ref.shape[0]
        n_rows = out_hbm.shape[0]
        half = even_ref.shape[1]
        copies = []
        for b in range(blocks):
            filtered = filter_block(x_ref, forward_ref, inverse_ref, response_ref, b, blocks, tiles, block)
            here = pl.ds(b * size, size)
            odd = dot(filtered, odd_table_ref[...])
            even = even_ref[here, :] + dot(filtered[:, (tiles - 1) * LANES :], even_table_ref[...])
            out_ref[here, :half] = (even + odd) * scale
            out_ref[here, half:] = (even - odd) * scale
            live = pl.ds(b * size, min(size, n_rows - b * size))
            copies.append(pltpu.make_async_copy(out_ref.at[live, :], out_hbm.at[live, :], sems.at[records + b]))
            copies[-1].start()
        for c in copies:
            c.wait()

    return kernel


def shards(traces, cable_depth, receiver, shot_slot, gather_home):
    records = lax.axis_size("shard")
    n_rec = gather_home.shape[0]
    per = n_rec // records
    n_channels, n_samples = traces.shape
    half = n_samples // 2
    block = 16 if records <= 16 else 8
    blocks = -(-(per + 1) // block)
    even_tiles, odd_tiles, mixed = bin_tiles()
    n_whole = len(even_tiles)
    last_tiles = odd_tiles + [mixed]
    rows = wave_rows(n_channels)
    wave = wave_table(n_channels)
    wave_t = np.ascontiguousarray(wave.T)
    weight = wave_weight(n_channels)
    even_table = time_table(n_samples, even_tiles + [mixed], 0)
    odd_table = time_table(n_samples, last_tiles, 1)
    pad_bins = np.zeros((HALF,), np.int64)
    placed_rows = records * blocks * block

    smem = pl.BlockSpec(memory_space=pltpu.SMEM)
    vmem = pl.BlockSpec(memory_space=pltpu.VMEM)
    hbm = pl.BlockSpec(memory_space=pl.ANY)
    params = pltpu.CompilerParams(vmem_limit_bytes=60 << 20)

    message_a, odd, mixed_part, place, energy = pl.pallas_call(
        front_kernel(per, blocks, block, n_whole),
        out_shape=(
            jax.ShapeDtypeStruct((records, n_whole * blocks, block, LANES), BF),
            jax.ShapeDtypeStruct((n_channels, half), BF),
            jax.ShapeDtypeStruct((n_channels, LANES), F32),
            jax.ShapeDtypeStruct((placed_rows, 2 * rows), BF),
            jax.ShapeDtypeStruct((1, LANES), F32),
        ),
        in_specs=[smem, vmem, vmem, vmem, vmem, hbm, hbm, vmem, vmem],
        out_specs=(vmem,) * 5,
        scratch_shapes=[
            pltpu.VMEM((n_channels, n_samples), F32),
            pltpu.VMEM(even_table.shape, BF),
            pltpu.VMEM((n_channels, n_whole * LANES), BF),
            pltpu.SemaphoreType.DMA((4,)),
        ],
        compiler_params=params,
        name="front",
    )(cable_depth, receiver.reshape(1, n_channels), gather_home.reshape(1, n_rec), vertical_table(n_channels, n_samples, even_tiles),
      weight, traces, even_table, wave, wave_t)
    arrived_a = lax.all_to_all(message_a, "shard", split_axis=0, concat_axis=0, tiled=True)

    message_b = pl.pallas_call(
        second_kernel(blocks, block, n_whole),
        out_shape=jax.ShapeDtypeStruct((records, (n_whole + 1) * blocks, block, LANES), BF),
        in_specs=[smem] + [vmem] * 8,
        out_specs=vmem,
        scratch_shapes=[pltpu.VMEM((n_channels, (n_whole + 1) * LANES), BF)],
        compiler_params=params,
        name="second",
    )(cable_depth, vertical_table(n_channels, n_samples, last_tiles + [pad_bins]), weight, odd, mixed_part, place, energy,
      odd_table, wave)
    arrived_b = lax.all_to_all(message_b, "shard", split_axis=0, concat_axis=0, tiled=True)

    forward = shot_forward(records, block)
    inverse = shot_inverse(records, block)
    size = records * block
    even = pl.pallas_call(
        even_kernel(blocks, block, n_whole),
        out_shape=jax.ShapeDtypeStruct((blocks * size, half), F32),
        in_specs=[smem, hbm] + [vmem] * 4,
        out_specs=vmem,
        scratch_shapes=[
            pltpu.VMEM((n_whole * blocks, size, LANES), BF),
            pltpu.SemaphoreType.DMA((records,)),
        ],
        compiler_params=params,
        name="even",
    )(shot_slot, arrived_a, forward, inverse, response_table(records, n_samples, even_tiles),
      np.ascontiguousarray(even_table[:, : n_whole * LANES].T))
    out = pl.pallas_call(
        last_kernel(blocks, block, n_whole + 1, n_channels * records),
        out_shape=jax.ShapeDtypeStruct((per * records, n_samples), F32),
        in_specs=[smem, hbm] + [vmem] * 6,
        out_specs=hbm,
        scratch_shapes=[
            pltpu.VMEM(((n_whole + 1) * blocks, size, LANES), BF),
            pltpu.VMEM((blocks * size, n_samples), F32),
            pltpu.SemaphoreType.DMA((records + blocks,)),
        ],
        compiler_params=params,
        name="last",
    )(shot_slot, arrived_b, forward, inverse, response_table(records, n_samples, last_tiles),
      np.ascontiguousarray(even_table[:, n_whole * LANES :].T), np.ascontiguousarray(odd_table.T), even)
    return out.reshape(per, records, n_samples)


def solution(mesh):
    in_specs = (
        P(("groups", "shard"), None),
        P(("groups", "shard")),
        P(("groups", "shard")),
        P("groups"),
        P("groups"),
    )
    out_specs = P(("groups", "shard"), None, None)
    return jax.shard_map(shards, mesh=mesh, in_specs=in_specs, out_specs=out_specs, check_vma=False)
```

```python
import math

import jax
import jax.numpy as jnp
import ml_dtypes
import numpy as np
from jax import lax
from jax.experimental import pallas as pl
from jax.experimental.pallas import tpu as pltpu
from jax.sharding import PartitionSpec as P

FREQ = 576

sample_step = 0.002
water_speed = 1500.0
channel_spacing = 12.5
shot_spacing = 25.0
surface_reflect = 0.9
ghost_floor = 0.1
reject_speed = 1500.0
low_floor = 4.0 * math.pi
energy_eps = 1e-06

BF = jnp.bfloat16
F32 = jnp.float32
LANES = 128
HALF = 64
ALL_VMEM = 60 << 20
PART_VMEM = 36 << 20


def to_bf16(table):
    return np.asarray(table, np.float32).astype(ml_dtypes.bfloat16)


def bin_tiles():
    even = np.arange(0, FREQ, 2)
    odd = np.arange(1, FREQ, 2)
    whole = len(even) // HALF
    left = len(even) - whole * HALF
    assert 2 * left == HALF and len(odd) == len(even)
    even_tiles = [even[j * HALF : (j + 1) * HALF] for j in range(whole)]
    odd_tiles = [odd[left + j * HALF : left + (j + 1) * HALF] for j in range(whole)]
    mixed = np.concatenate([even[whole * HALF :], odd[:left]])
    return even_tiles, odd_tiles, mixed


def time_table(n_samples, tiles, parity):
    samples = np.arange(n_samples // 2, dtype=np.int64)
    parts = []
    for bins in tiles:
        angle = (samples[:, None] * bins[None, :] % n_samples) * (2.0 * np.pi / n_samples)
        keep = (bins % 2 == parity).astype(np.float64)[None, :]
        parts += [np.cos(angle) * keep, -np.sin(angle) * keep]
    return to_bf16(np.concatenate(parts, axis=1))


def wave_rows(n_channels):
    return -(-(n_channels // 2 + 1) // 16) * 16


def wave_table(n_channels):
    rows = wave_rows(n_channels)
    k = np.arange(rows, dtype=np.int64)
    c = np.arange(n_channels, dtype=np.int64)
    angle = (k[:, None] * c[None, :] % n_channels) * (2.0 * np.pi / n_channels)
    live = (k <= n_channels // 2)[:, None]
    inner = ((k > 0) & (2 * k < n_channels))[:, None]
    return to_bf16(np.concatenate([np.cos(angle) * live, np.sin(angle) * inner], axis=0))


def vertical_table(n_channels, n_samples, tiles):
    rows = wave_rows(n_channels)
    k = np.minimum(np.arange(rows), n_channels // 2).astype(np.float64)
    kx = 2.0 * np.pi * k / (n_channels * channel_spacing)
    bins = np.concatenate(tiles).astype(np.float64)
    slow = 2.0 * np.pi * bins / (n_samples * sample_step) / water_speed
    return (2.0 * np.sqrt(np.maximum(slow[None, :] ** 2 - kx[:, None] ** 2, 0.0))).astype(np.float32)


def wave_weight(n_channels):
    rows = wave_rows(n_channels)
    k = np.arange(rows)
    single = (k == 0) | (2 * k == n_channels)
    weight = np.where(single, 1.0, 2.0) / n_channels
    return np.repeat(weight[:, None], LANES, axis=1).astype(np.float32)


def shot_basis(records):
    k = np.concatenate([np.arange(records + 1), np.arange(1, records)])
    p = np.arange(records)
    angle = (k[:, None] * p[None, :] % (2 * records)) * (np.pi / records)
    is_sin = (np.arange(2 * records) > records)[:, None]
    return np.where(is_sin, np.sin(angle), np.cos(angle)), k


def shot_forward(records, block):
    basis, _ = shot_basis(records)
    full = np.einsum("kp,gh->gkph", basis, np.eye(block))
    return to_bf16(full.reshape(block * 2 * records, records * block))


def shot_inverse(records, block):
    basis, _ = shot_basis(records)
    full = np.einsum("kp,gh->gphk", basis, np.eye(block))
    return to_bf16(full.reshape(block * records, block * 2 * records))


def response_table(records, n_samples, tiles):
    _, k = shot_basis(records)
    single = (k == 0) | (k == records)
    parts = []
    for bins in tiles:
        angular = 2.0 * np.pi * bins.astype(np.float64) / (n_samples * sample_step)
        shot_number = 2.0 * np.pi * k / (2 * records * shot_spacing)
        ratio = reject_speed * shot_number[:, None] / (angular[None, :] + low_floor)
        value = 1.0 / (1.0 + ratio**4) / (2.0 * records)
        value = value * np.where(single, 1.0, 2.0)[:, None] * np.where(bins == 0, 1.0, 2.0)[None, :]
        parts += [value, value]
    return np.concatenate(parts, axis=1).astype(np.float32)


def sin_cos(angle):
    turns = jnp.floor(angle * (2.0 / math.pi) + 0.5)
    rest = ((angle - turns * 1.5703125) - turns * 4.837512969970703125e-4) - turns * 7.54978995489188216e-8
    sq = rest * rest
    sine = ((-1.9515295891e-4 * sq + 8.3321608736e-3) * sq - 1.6666654611e-1) * sq * rest + rest
    cosine = ((2.443315711809948e-5 * sq - 1.388731625493765e-3) * sq + 4.166664568298827e-2) * sq * sq - 0.5 * sq + 1.0
    quarter = turns.astype(jnp.int32)
    odd = (quarter & 1) == 1
    sin_out = jnp.where(odd, cosine, sine)
    cos_out = jnp.where(odd, sine, cosine)
    sin_out = jnp.where((quarter & 2) == 2, -sin_out, sin_out)
    cos_out = jnp.where(((quarter + 1) & 2) == 2, -cos_out, cos_out)
    return sin_out, cos_out


def gains(vertical, depth, weight):
    sine, cosine = sin_cos(vertical * depth)
    denominator = 1.0 - 2.0 * surface_reflect * cosine + surface_reflect * surface_reflect + ghost_floor
    scale = weight / denominator
    return (1.0 - surface_reflect * cosine) * scale, -surface_reflect * sine * scale


def tile_gains(gain_re, gain_im, second):
    lane = lax.broadcasted_iota(jnp.int32, gain_re.shape, 1)
    low = lane < HALF
    re_other = pltpu.roll(gain_re, HALF, 1)
    im_other = pltpu.roll(gain_im, HALF, 1)
    if second:
        return jnp.where(low, re_other, gain_re), jnp.where(low, -im_other, gain_im)
    return jnp.where(low, gain_re, re_other), jnp.where(low, -gain_im, im_other)


def dot(a, b):
    return jnp.dot(a, b, preferred_element_type=F32)


def lift_and_place(spec_pair, n_tiles, vertical, depth, weight, wave_ref, place_ref, rows):
    plain = dot(wave_ref[...], spec_pair)
    gain_re, gain_im = gains(vertical, depth, weight)
    lifted = []
    for t in range(n_tiles):
        same, swapped = tile_gains(gain_re, gain_im, t == 1)
        both = []
        for h in range(2):
            part = plain[h * rows : (h + 1) * rows, t * LANES : (t + 1) * LANES]
            both.append((part * same + pltpu.roll(part, HALF, 1) * swapped).astype(BF))
        lifted.append(jnp.concatenate(both, axis=0))
    lifted = lifted[0] if n_tiles == 1 else jnp.concatenate(lifted, axis=1)
    return dot(place_ref[...], lifted)


def energy_of(placed):
    total = jnp.sum(placed * placed, axis=0, keepdims=True)
    return sum(total[:, t * LANES : (t + 1) * LANES] for t in range(placed.shape[1] // LANES))


def store_message(stores, placed, first_tile, blocks, block):
    size = blocks * block
    for t in range(placed.shape[1] // LANES):
        tile = placed[:, t * LANES : (t + 1) * LANES].astype(BF)
        here = pl.ds((first_tile + t) * blocks, blocks)
        for m, store in enumerate(stores):
            store(here, tile[m * size : (m + 1) * size].reshape(blocks, block, LANES))


def into(ref, index=None):
    def store(here, value):
        if index is None:
            ref[here, :, :] = value
        else:
            ref[index, here, :, :] = value

    return store


def split_energy(energy):
    total = jnp.sum(energy, axis=1, keepdims=True)
    high = total.astype(BF).astype(F32)
    middle = (total - high).astype(BF).astype(F32)
    low = total - high - middle
    lane = lax.broadcasted_iota(jnp.int32, (1, LANES), 1)
    return jnp.where(lane == 0, high, jnp.where(lane == 1, middle, jnp.where(lane == 2, low, 0.0)))


def partners(records):
    order = [0]
    span = records // 2
    while span:
        order += range(span, 2 * span)
        span //= 2
    return order


def front_kernel(per, blocks, block, n_whole, records):
    def kernel(depth_ref, receiver_ref, home_ref, traces_hbm, wave_t_hbm, table_hbm, vertical_hbm, wave_hbm, weight_hbm,
               message_ref, odd_hbm, mixed_hbm, place_hbm, energy_ref,
               traces_ref, wave_t_ref, table_ref, vertical_ref, wave_ref, weight_ref, spec_ref, odd_ref, mixed_ref, place_ref, sems):
        me = lax.axis_index("shard")
        n_channels, n_samples = traces_ref.shape
        half = n_samples // 2
        steps = 3
        step = n_channels // steps
        pairs = [(traces_hbm.at[pl.ds(s * step, step), :], traces_ref.at[pl.ds(s * step, step), :]) for s in range(steps)]
        pairs = [(wave_t_hbm, wave_t_ref), pairs[0], (table_hbm, table_ref), *pairs[1:], (vertical_hbm, vertical_ref),
                 (weight_hbm, weight_ref), (wave_hbm, wave_ref)]
        copies = [pltpu.make_async_copy(a, b, sems.at[i]) for i, (a, b) in enumerate(pairs)]
        for c in copies:
            c.start()
        rows = wave_ref.shape[0] // 2
        n_rec = home_ref.shape[0]
        padded = blocks * block
        home = home_ref[...].reshape(1, n_rec)
        device = jnp.floor((home.astype(F32) + 0.5) * (1.0 / per)).astype(jnp.int32)
        home_row = (device ^ me) * padded + (home - device * per)
        to_home = lax.broadcasted_iota(jnp.int32, (records * padded, n_rec), 0) == home_row
        to_home = jnp.where(to_home, 1.0, 0.0).astype(BF)
        to_bin = lax.broadcasted_iota(jnp.int32, (n_rec, n_channels), 0) == receiver_ref[...].reshape(1, n_channels)
        to_bin = jnp.where(to_bin, 1.0, 0.0).astype(BF)
        picked = dot(to_home, to_bin).astype(BF)
        copies[0].wait()
        place_ref[...] = dot(picked, wave_t_ref[...]).astype(BF)
        first_out = len(copies)
        outs = [pltpu.make_async_copy(place_ref, place_hbm, sems.at[first_out])]
        outs[0].start()
        for s in range(steps):
            copies[1 if s == 0 else s + 2].wait()
            if s == 0:
                copies[2].wait()
            part = pl.ds(s * step, step)
            first = traces_ref[part, :half]
            second = traces_ref[part, half:]
            odd_ref[part, :] = (first - second).astype(BF)
            got = dot((first + second).astype(BF), table_ref[...])
            spec_ref[part, :] = got[:, : n_whole * LANES].astype(BF)
            mixed_ref[part, :] = got[:, n_whole * LANES :]
        for a, b in ((odd_ref, odd_hbm), (mixed_ref, mixed_hbm)):
            outs.append(pltpu.make_async_copy(a, b, sems.at[first_out + len(outs)]))
            outs[-1].start()
        for c in copies[steps + 2 :]:
            c.wait()
        energy = jnp.zeros((1, LANES), F32)
        stores = [into(message_ref, me ^ m) for m in range(records)]
        for pair in range(n_whole // 2):
            cols = slice(2 * pair * LANES, (2 * pair + 2) * LANES)
            placed = lift_and_place(spec_ref[:, cols], 2, vertical_ref[:, pair * LANES : (pair + 1) * LANES], depth_ref[0],
                                    weight_ref[...], wave_ref, place_ref, rows)
            energy = energy + energy_of(placed)
            store_message(stores, placed, 2 * pair, blocks, block)
        energy_ref[...] = energy
        for c in outs:
            c.wait()

    return kernel


def second_kernel(blocks, block, n_whole, records, one_message):
    def kernel(depth_ref, energy_ref, odd_hbm, table_hbm, mixed_hbm, wave_hbm, vertical_hbm, weight_hbm, place_hbm, *refs):
        *messages, odd_ref, table_ref, mixed_ref, wave_ref, vertical_ref, weight_ref, place_ref, spec_ref, sems = refs
        pairs = [(odd_hbm, odd_ref), (table_hbm, table_ref), (mixed_hbm, mixed_ref), (wave_hbm, wave_ref),
                 (vertical_hbm, vertical_ref), (weight_hbm, weight_ref), (place_hbm, place_ref)]
        copies = [pltpu.make_async_copy(a, b, sems.at[i]) for i, (a, b) in enumerate(pairs)]
        for c in copies:
            c.start()
        me = lax.axis_index("shard")
        rows = wave_ref.shape[0] // 2
        for c in copies[:3]:
            c.wait()
        got = dot(odd_ref[...], table_ref[...])
        whole = n_whole * LANES
        spec_ref[:, :whole] = got[:, :whole].astype(BF)
        spec_ref[:, whole:] = (got[:, whole:] + mixed_ref[...]).astype(BF)
        for c in copies[3:]:
            c.wait()
        energy = energy_ref[...]
        if one_message:
            stores = [into(messages[0], me ^ m) for m in range(records)]
        else:
            stores = [into(messages[partners(records).index(m)]) for m in range(records)]
        for pair in reversed(range(n_whole // 2 + 1)):
            n_tiles = 2 if pair < n_whole // 2 else 1
            cols = slice(2 * pair * LANES, (2 * pair + n_tiles) * LANES)
            placed = lift_and_place(spec_ref[:, cols], n_tiles, vertical_ref[:, pair * LANES : (pair + 1) * LANES], depth_ref[0],
                                    weight_ref[...], wave_ref, place_ref, rows)
            energy = energy + energy_of(placed)
            if pair == 0:
                size = blocks * block
                row = lax.broadcasted_iota(jnp.int32, (records * size, LANES), 0)
                first = jnp.where(row % size == size - 1, split_energy(energy), placed[:, :LANES])
                placed = jnp.concatenate([first, placed[:, LANES:]], axis=1)
            store_message(stores, placed, 2 * pair, blocks, block)

    return kernel


def arrive(slot_ref, sources, x_ref, sems, block):
    copies = []
    for i, (record, ref) in enumerate(sources):
        at = pl.multiple_of(slot_ref[record] * block, block)
        copies.append(pltpu.make_async_copy(ref, x_ref.at[:, pl.ds(at, block), :], sems.at[i]))
    for c in copies:
        c.start()
    for c in copies:
        c.wait()


def filter_block(x_ref, forward_ref, inverse_ref, response_ref, b, blocks, tiles, block):
    out = []
    k = response_ref.shape[0]
    for first in range(0, tiles, 2):
        n = min(2, tiles - first)
        x = [x_ref[(first + t) * blocks + b] for t in range(n)]
        x = x[0] if n == 1 else jnp.concatenate(x, axis=1)
        part = dot(forward_ref[...], x).reshape(block, k, n * LANES)
        part = part * response_ref[:, first * LANES : (first + n) * LANES][None]
        part = part.reshape(block * k, n * LANES).astype(BF)
        out.append(dot(inverse_ref[...], part).astype(BF))
    return out[0] if len(out) == 1 else jnp.concatenate(out, axis=1)


def even_kernel(blocks, block, tiles):
    def kernel(slot_ref, arrived_ref, forward_hbm, inverse_hbm, response_hbm, table_hbm, response_b_hbm, even_b_hbm, odd_b_hbm,
               out_ref, forward_ref, inverse_ref, response_b_ref, even_b_ref, odd_b_ref, x_ref, response_ref, table_ref, sems):
        pairs = [(forward_hbm, forward_ref), (inverse_hbm, inverse_ref), (response_hbm, response_ref), (table_hbm, table_ref),
                 (response_b_hbm, response_b_ref), (even_b_hbm, even_b_ref), (odd_b_hbm, odd_b_ref)]
        records = arrived_ref.shape[0]
        copies = [pltpu.make_async_copy(a, b, sems.at[records + i]) for i, (a, b) in enumerate(pairs)]
        for c in copies:
            c.start()
        arrive(slot_ref, [(s, arrived_ref.at[s]) for s in range(records)], x_ref, sems, block)
        for c in copies:
            c.wait()
        size = inverse_ref.shape[0]
        for b in range(blocks):
            filtered = filter_block(x_ref, forward_ref, inverse_ref, response_ref, b, blocks, tiles, block)
            out_ref[pl.ds(b * size, size), :] = dot(filtered, table_ref[...])

    return kernel


def last_kernel(blocks, block, tiles, n_traces, records, one_message):
    def kernel(slot_ref, forward_ref, inverse_ref, response_ref, even_table_ref, odd_table_ref, even_ref, *refs):
        out_hbm, x_ref, out_ref, sems = refs[-4:]
        arrived = refs[:-4]
        if one_message:
            sources = [(s, arrived[0].at[s]) for s in range(records)]
        else:
            me = lax.axis_index("shard")
            sources = [(me ^ m, ref) for m, ref in zip(partners(records), arrived)]
        arrive(slot_ref, sources, x_ref, sems, block)
        ends = x_ref[blocks - 1].astype(F32).reshape(records, block, LANES)
        row = lax.broadcasted_iota(jnp.int32, ends.shape, 1)
        lane = lax.broadcasted_iota(jnp.int32, ends.shape, 2)
        ends = jnp.where((row == block - 1) & (lane < 3), ends, 0.0)
        energy = jnp.sum(jnp.sum(ends, axis=0), keepdims=True)
        scale = lax.rsqrt(2.0 * FREQ * (energy * (1.0 / (n_traces * FREQ)) + energy_eps))
        size = inverse_ref.shape[0]
        n_rows = out_hbm.shape[0]
        half = even_ref.shape[1]
        copies = []
        for b in range(blocks):
            filtered = filter_block(x_ref, forward_ref, inverse_ref, response_ref, b, blocks, tiles, block)
            here = pl.ds(b * size, size)
            odd = dot(filtered, odd_table_ref[...])
            even = even_ref[here, :] + dot(filtered[:, (tiles - 1) * LANES :], even_table_ref[...])
            out_ref[here, :half] = (even + odd) * scale
            out_ref[here, half:] = (even - odd) * scale
            live = pl.ds(b * size, min(size, n_rows - b * size))
            copies.append(pltpu.make_async_copy(out_ref.at[live, :], out_hbm.at[live, :], sems.at[records + b]))
            copies[-1].start()
        for c in copies:
            c.wait()

    return kernel


def shards(traces, cable_depth, receiver, shot_slot, gather_home):
    records = lax.axis_size("shard")
    n_rec = gather_home.shape[0]
    per = n_rec // records
    n_channels, n_samples = traces.shape
    half = n_samples // 2
    block = 16 if records <= 16 else 8
    blocks = -(-(per + 1) // block)
    even_tiles, odd_tiles, mixed = bin_tiles()
    n_whole = len(even_tiles)
    last_tiles = odd_tiles + [mixed]
    rows = wave_rows(n_channels)
    wave = wave_table(n_channels)
    wave_t = np.ascontiguousarray(wave.T)
    weight = wave_weight(n_channels)
    even_table = time_table(n_samples, even_tiles + [mixed], 0)
    odd_table = time_table(n_samples, last_tiles, 1)
    pad_bins = np.zeros((HALF,), np.int64)
    placed_rows = records * blocks * block

    smem = pl.BlockSpec(memory_space=pltpu.SMEM)
    vmem = pl.BlockSpec(memory_space=pltpu.VMEM)
    hbm = pl.BlockSpec(memory_space=pltpu.HBM)
    alone = pltpu.CompilerParams(vmem_limit_bytes=ALL_VMEM)
    shared = pltpu.CompilerParams(vmem_limit_bytes=PART_VMEM)
    pairwise = records <= 16
    vertical = vertical_table(n_channels, n_samples, even_tiles)
    vertical_b = vertical_table(n_channels, n_samples, last_tiles + [pad_bins])

    def scratch(array):
        return pltpu.VMEM(array.shape, array.dtype)

    message_a, odd, mixed_part, place, energy = pl.pallas_call(
        front_kernel(per, blocks, block, n_whole, records),
        out_shape=(
            jax.ShapeDtypeStruct((records, n_whole * blocks, block, LANES), BF),
            jax.ShapeDtypeStruct((n_channels, half), BF),
            jax.ShapeDtypeStruct((n_channels, LANES), F32),
            jax.ShapeDtypeStruct((placed_rows, 2 * rows), BF),
            jax.ShapeDtypeStruct((1, LANES), F32),
        ),
        in_specs=[smem, vmem, vmem] + [hbm] * 6,
        out_specs=(vmem, hbm, hbm, hbm, vmem),
        scratch_shapes=[
            pltpu.VMEM((n_channels, n_samples), F32),
            scratch(wave_t),
            scratch(even_table),
            scratch(vertical),
            scratch(wave),
            scratch(weight),
            pltpu.VMEM((n_channels, n_whole * LANES), BF),
            pltpu.VMEM((n_channels, half), BF),
            pltpu.VMEM((n_channels, LANES), F32),
            pltpu.VMEM((placed_rows, 2 * rows), BF),
            pltpu.SemaphoreType.DMA((11,)),
        ],
        compiler_params=alone,
        name="front",
    )(cable_depth, receiver, gather_home, traces, wave_t, even_table, vertical, wave, weight)
    arrived_a = lax.all_to_all(message_a, "shard", split_axis=0, concat_axis=0, tiled=True)

    shape_b = ((n_whole + 1) * blocks, block, LANES)
    if pairwise:
        shapes_b = tuple(jax.ShapeDtypeStruct(shape_b, BF) for _ in range(records))
    else:
        shapes_b = (jax.ShapeDtypeStruct((records, *shape_b), BF),)
    messages = pl.pallas_call(
        second_kernel(blocks, block, n_whole, records, not pairwise),
        out_shape=shapes_b,
        in_specs=[smem, vmem] + [hbm] * 7,
        out_specs=(vmem,) * len(shapes_b),
        scratch_shapes=[
            scratch(odd),
            scratch(odd_table),
            scratch(mixed_part),
            scratch(wave),
            scratch(vertical_b),
            scratch(weight),
            scratch(place),
            pltpu.VMEM((n_channels, (n_whole + 1) * LANES), BF),
            pltpu.SemaphoreType.DMA((7,)),
        ],
        compiler_params=alone,
        name="second",
    )(cable_depth, energy, odd, odd_table, mixed_part, wave, vertical_b, weight, place)
    if pairwise:
        arrived_b = [messages[0]]
        for m, message in list(zip(partners(records), messages))[1:]:
            arrived_b.append(lax.ppermute(message, "shard", [(s, s ^ m) for s in range(records)]))
    else:
        arrived_b = [lax.all_to_all(messages[0], "shard", split_axis=0, concat_axis=0, tiled=True)]

    forward = shot_forward(records, block)
    inverse = shot_inverse(records, block)
    size = records * block
    response = response_table(records, n_samples, even_tiles)
    response_b = response_table(records, n_samples, last_tiles)
    even_a = np.ascontiguousarray(even_table[:, : n_whole * LANES].T)
    even_b = np.ascontiguousarray(even_table[:, n_whole * LANES :].T)
    odd_b = np.ascontiguousarray(odd_table.T)
    even, *kept = pl.pallas_call(
        even_kernel(blocks, block, n_whole),
        out_shape=(
            pltpu.VMEM((blocks * size, half), F32),
            scratch(forward),
            scratch(inverse),
            scratch(response_b),
            scratch(even_b),
            scratch(odd_b),
        ),
        in_specs=[smem, vmem] + [hbm] * 7,
        out_specs=(vmem,) * 6,
        scratch_shapes=[
            pltpu.VMEM((n_whole * blocks, size, LANES), BF),
            pltpu.VMEM(response.shape, F32),
            pltpu.VMEM(even_a.shape, BF),
            pltpu.SemaphoreType.DMA((records + 7,)),
        ],
        compiler_params=shared,
        name="even",
    )(shot_slot, arrived_a, forward, inverse, response, even_a, response_b, even_b, odd_b)
    out = pl.pallas_call(
        last_kernel(blocks, block, n_whole + 1, n_channels * records, records, not pairwise),
        out_shape=jax.ShapeDtypeStruct((per * records, n_samples), F32),
        in_specs=[smem] + [vmem] * (6 + len(arrived_b)),
        out_specs=hbm,
        scratch_shapes=[
            pltpu.VMEM(((n_whole + 1) * blocks, size, LANES), BF),
            pltpu.VMEM((blocks * size, n_samples), F32),
            pltpu.SemaphoreType.DMA((records + blocks,)),
        ],
        compiler_params=shared,
        name="last",
    )(shot_slot, *kept, even, *arrived_b)
    return out.reshape(per, records, n_samples)


def solution(mesh):
    in_specs = (
        P(("groups", "shard"), None),
        P(("groups", "shard")),
        P(("groups", "shard")),
        P("groups"),
        P("groups"),
    )
    out_specs = P(("groups", "shard"), None, None)
    return jax.shard_map(shards, mesh=mesh, in_specs=in_specs, out_specs=out_specs, check_vma=False)
```

```python
import math

import jax
import jax.numpy as jnp
import ml_dtypes
import numpy as np
from jax import lax
from jax.experimental import pallas as pl
from jax.experimental.pallas import tpu as pltpu
from jax.sharding import PartitionSpec as P

FREQ = 576

sample_step = 0.002
water_speed = 1500.0
channel_spacing = 12.5
shot_spacing = 25.0
surface_reflect = 0.9
ghost_floor = 0.1
reject_speed = 1500.0
low_floor = 4.0 * math.pi
energy_eps = 1e-06

BF = jnp.bfloat16
F32 = jnp.float32
LANES = 128
HALF = 64
UNIT = 8
ALL_VMEM = 60 << 20
PART_VMEM = 36 << 20


def to_bf16(table):
    return np.asarray(table, np.float32).astype(ml_dtypes.bfloat16)


def bin_tiles():
    even = np.arange(0, FREQ, 2)
    odd = np.arange(1, FREQ, 2)
    whole = len(even) // HALF
    left = len(even) - whole * HALF
    assert 2 * left == HALF and len(odd) == len(even)
    even_tiles = [even[j * HALF : (j + 1) * HALF] for j in range(whole)]
    odd_tiles = [odd[left + j * HALF : left + (j + 1) * HALF] for j in range(whole)]
    mixed = np.concatenate([even[whole * HALF :], odd[:left]])
    return even_tiles, odd_tiles, mixed


def time_table(n_samples, tiles, parity):
    samples = np.arange(n_samples // 2, dtype=np.int64)
    parts = []
    for bins in tiles:
        angle = (samples[:, None] * bins[None, :] % n_samples) * (2.0 * np.pi / n_samples)
        keep = (bins % 2 == parity).astype(np.float64)[None, :]
        parts += [np.cos(angle) * keep, -np.sin(angle) * keep]
    return to_bf16(np.concatenate(parts, axis=1))


def wave_rows(n_channels):
    return -(-(n_channels // 2 + 1) // 16) * 16


def wave_table(n_channels):
    rows = wave_rows(n_channels)
    k = np.arange(rows, dtype=np.int64)
    c = np.arange(n_channels, dtype=np.int64)
    angle = (k[:, None] * c[None, :] % n_channels) * (2.0 * np.pi / n_channels)
    live = (k <= n_channels // 2)[:, None]
    inner = ((k > 0) & (2 * k < n_channels))[:, None]
    return to_bf16(np.concatenate([np.cos(angle) * live, np.sin(angle) * inner], axis=0))


def vertical_table(n_channels, n_samples, tiles):
    rows = wave_rows(n_channels)
    k = np.minimum(np.arange(rows), n_channels // 2).astype(np.float64)
    kx = 2.0 * np.pi * k / (n_channels * channel_spacing)
    bins = np.concatenate(tiles).astype(np.float64)
    slow = 2.0 * np.pi * bins / (n_samples * sample_step) / water_speed
    return (2.0 * np.sqrt(np.maximum(slow[None, :] ** 2 - kx[:, None] ** 2, 0.0))).astype(np.float32)


def shot_basis(records):
    k = np.concatenate([np.arange(records + 1), np.arange(1, records)])
    p = np.arange(records)
    angle = (k[:, None] * p[None, :] % (2 * records)) * (np.pi / records)
    is_sin = (np.arange(2 * records) > records)[:, None]
    return np.where(is_sin, np.sin(angle), np.cos(angle)), k


def shot_forward(records, block):
    basis, _ = shot_basis(records)
    full = np.einsum("kp,gh->gkph", basis, np.eye(block))
    return to_bf16(full.reshape(block * 2 * records, records * block))


def shot_inverse(records):
    basis, _ = shot_basis(records)
    full = np.einsum("kp,gh->gphk", basis, np.eye(UNIT))
    return to_bf16(full.reshape(UNIT * records, UNIT * 2 * records))


def response_table(records, n_samples, tiles):
    _, k = shot_basis(records)
    single = (k == 0) | (k == records)
    parts = []
    for bins in tiles:
        angular = 2.0 * np.pi * bins.astype(np.float64) / (n_samples * sample_step)
        shot_number = 2.0 * np.pi * k / (2 * records * shot_spacing)
        ratio = reject_speed * shot_number[:, None] / (angular[None, :] + low_floor)
        value = 1.0 / (1.0 + ratio**4) / (2.0 * records)
        value = value * np.where(single, 1.0, 2.0)[:, None] * np.where(bins == 0, 1.0, 2.0)[None, :]
        parts += [value, value]
    return np.concatenate(parts, axis=1).astype(np.float32)


def sin_cos(angle):
    turns = jnp.floor(angle * (2.0 / math.pi) + 0.5)
    rest = ((angle - turns * 1.5703125) - turns * 4.837512969970703125e-4) - turns * 7.54978995489188216e-8
    sq = rest * rest
    sine = ((-1.9515295891e-4 * sq + 8.3321608736e-3) * sq - 1.6666654611e-1) * sq * rest + rest
    cosine = ((2.443315711809948e-5 * sq - 1.388731625493765e-3) * sq + 4.166664568298827e-2) * sq * sq - 0.5 * sq + 1.0
    quarter = turns.astype(jnp.int32)
    odd = (quarter & 1) == 1
    sin_out = jnp.where(odd, cosine, sine)
    cos_out = jnp.where(odd, sine, cosine)
    sin_out = jnp.where((quarter & 2) == 2, -sin_out, sin_out)
    cos_out = jnp.where(((quarter + 1) & 2) == 2, -cos_out, cos_out)
    return sin_out, cos_out


def gains(vertical, depth, weight):
    sine, cosine = sin_cos(vertical * depth)
    denominator = 1.0 - 2.0 * surface_reflect * cosine + surface_reflect * surface_reflect + ghost_floor
    scale = weight / denominator
    return (1.0 - surface_reflect * cosine) * scale, -surface_reflect * sine * scale


def tile_gains(gain_re, gain_im, second):
    lane = lax.broadcasted_iota(jnp.int32, gain_re.shape, 1)
    low = lane < HALF
    re_other = pltpu.roll(gain_re, HALF, 1)
    im_other = pltpu.roll(gain_im, HALF, 1)
    if second:
        return jnp.where(low, re_other, gain_re), jnp.where(low, -im_other, gain_im)
    return jnp.where(low, gain_re, re_other), jnp.where(low, -gain_im, im_other)


def dot(a, b):
    return jnp.dot(a, b, preferred_element_type=F32)


def lift(spec, factors_ref, first, wave_ref):
    rows = wave_ref.shape[0] // 2
    plain = dot(wave_ref[...], spec)
    lifted = []
    for t in range(spec.shape[1] // LANES):
        same = factors_ref[0, first + t]
        swapped = factors_ref[1, first + t]
        both = []
        for h in range(2):
            part = plain[h * rows : (h + 1) * rows, t * LANES : (t + 1) * LANES]
            both.append((part * same + pltpu.roll(part, HALF, 1) * swapped).astype(BF))
        lifted.append(jnp.concatenate(both, axis=0))
    return join(lifted)


def store_factors(factors_ref, vertical_ref, depth, n_channels):
    tiles = factors_ref.shape[1]
    row = lax.broadcasted_iota(jnp.int32, (vertical_ref.shape[0], LANES), 0)
    single = (row == 0) | (row * 2 == n_channels)
    weight = jnp.where(single, 1.0 / n_channels, 2.0 / n_channels)
    for t in range(0, tiles, 2):
        gain_re, gain_im = gains(vertical_ref[:, t * HALF : (t + 2) * HALF], depth, weight)
        for h in range(min(2, tiles - t)):
            factors_ref[0, t + h], factors_ref[1, t + h] = tile_gains(gain_re, gain_im, h == 1)


def join(parts):
    return parts[0] if len(parts) == 1 else jnp.concatenate(parts, axis=1)


def energy_of(cleaned):
    total = jnp.sum(cleaned * cleaned, axis=0, keepdims=True)
    return sum(total[:, t * LANES : (t + 1) * LANES] for t in range(cleaned.shape[1] // LANES))


class Layout:
    def __init__(self, per, tiles, spare):
        self.whole = per // UNIT
        self.left = per % UNIT
        self.tiles = tiles
        self.shared = UNIT // self.left if self.left else 1
        rows = tiles * self.left
        self.left_units = -(-tiles // self.shared) if self.left else 0
        if spare and rows - (self.left_units - 1) * self.shared * self.left == UNIT or spare and not self.left_units:
            self.left_units += 1
        self.units = self.whole * tiles + self.left_units

    def unit(self, tile, u):
        if u < self.whole:
            return tile * self.whole + u, 0
        if u == self.whole and self.left:
            return self.whole * self.tiles + tile // self.shared, tile % self.shared * self.left
        return None, 0


def partner(me, dz, lo, n, sign):
    return (me // 4 + (dz if sign > 0 else n - dz)) % n * 4 + ((me % 4) ^ lo)


def partners(records):
    n = records // 4
    far = sorted(range(1, n), key=lambda d: -min(d, n - d))
    return [0] + [4 * dz + lo for dz in far for lo in range(4)] + [1, 2, 3]


def place_message(placed, layout, frame, store, i, energy=None):
    mine = placed[i * frame : (i + 1) * frame]
    parts = [mine[: layout.whole * UNIT, t * LANES : (t + 1) * LANES] for t in range(layout.tiles)] if layout.whole else []
    left = [jnp.zeros((UNIT, LANES), F32) for _ in range(layout.left_units)]
    if layout.left:
        row = lax.broadcasted_iota(jnp.int32, (UNIT, LANES), 0)
        for t in range(layout.tiles):
            unit = mine[layout.whole * UNIT : (layout.whole + 1) * UNIT, t * LANES : (t + 1) * LANES]
            shift = t % layout.shared * layout.left
            unit = jnp.where(row < layout.left, unit, 0.0)
            left[t // layout.shared] += pltpu.roll(unit, shift, 0) if shift else unit
    if energy is not None:
        row = lax.broadcasted_iota(jnp.int32, (UNIT, LANES), 0)
        left[-1] = jnp.where(row == UNIT - 1, energy, left[-1])
    store(jnp.concatenate(parts + left, axis=0).astype(BF))


def split_energy(energy):
    total = jnp.sum(energy, axis=1, keepdims=True)
    high = total.astype(BF).astype(F32)
    middle = (total - high).astype(BF).astype(F32)
    low = total - high - middle
    lane = lax.broadcasted_iota(jnp.int32, (1, LANES), 1)
    return jnp.where(lane == 0, high, jnp.where(lane == 1, middle, jnp.where(lane == 2, low, 0.0)))


def into(ref, index=None):
    def store(value):
        if index is None:
            ref[...] = value
        else:
            ref[index] = value

    return store


def start_all(pairs, sems, first=0):
    copies = [pltpu.make_async_copy(a, b, sems.at[first + i]) for i, (a, b) in enumerate(pairs)]
    for c in copies:
        c.start()
    return copies


def front_kernel(per, frame, layout, records):
    def kernel(depth_ref, receiver_ref, home_ref, vertical_hbm, wave_t_hbm, traces_hbm, table_hbm, wave_hbm,
               message_ref, sums_hbm, place_hbm, energy_ref,
               vertical_ref, wave_t_ref, traces_ref, table_ref, wave_ref, sums_ref, place_ref, placed_ref, factors_ref, sems):
        me = lax.axis_index("shard")
        n_channels, n_samples = traces_ref.shape
        half = n_samples // 2
        steps = 3
        step = n_channels // steps
        pairs = [(traces_hbm.at[pl.ds(s * step, step), :], traces_ref.at[pl.ds(s * step, step), :]) for s in range(steps)]
        pairs = [(vertical_hbm, vertical_ref), (wave_t_hbm, wave_t_ref), *pairs, (table_hbm, table_ref), (wave_hbm, wave_ref)]
        copies = start_all(pairs, sems)
        n_rec = home_ref.shape[0]
        home = home_ref[...].reshape(1, n_rec)
        device = jnp.floor((home.astype(F32) + 0.5) * (1.0 / per)).astype(jnp.int32)
        n = records // 4
        turn = (device >> 2) - me // 4
        turn = jnp.where(turn < 0, turn + n, turn)
        home_row = (turn * 4 + ((device & 3) ^ (me % 4))) * frame + (home - device * per)
        both = jnp.concatenate([home_row >> 7, home_row & 127, jnp.zeros((14, n_rec), jnp.int32)], axis=0).astype(F32).astype(BF)
        to_bin = lax.broadcasted_iota(jnp.int32, (n_rec, n_channels), 0) == receiver_ref[...].reshape(1, n_channels)
        target = dot(both, jnp.where(to_bin, 1.0, 0.0).astype(BF))
        target = (target[0:1] * 128.0 + target[1:2]).astype(jnp.int32)
        picked = lax.broadcasted_iota(jnp.int32, (records * frame, n_channels), 0) == target
        picked = jnp.where(picked, 1.0, 0.0).astype(BF)
        copies[0].wait()
        copies[1].wait()
        place_ref[...] = dot(picked, wave_t_ref[...]).astype(BF)
        store_factors(factors_ref, vertical_ref, depth_ref[0], n_channels)
        outs = start_all([(place_ref, place_hbm)], sems, len(copies))
        for s in range(steps):
            copies[2 + s].wait()
            part = pl.ds(s * step, step)
            first = traces_ref[part, :half]
            second = traces_ref[part, half:]
            sums_ref[part, :half] = (first + second).astype(BF)
            sums_ref[part, half:] = (first - second).astype(BF)
        outs += start_all([(sums_ref, sums_hbm)], sems, len(copies) + 1)
        copies[-2].wait()
        spec = dot(sums_ref[:, :half], table_ref[...]).astype(BF)
        copies[-1].wait()
        placed_ref[...] = dot(place_ref[...], lift(spec, factors_ref, 0, wave_ref))
        energy_ref[...] = energy_of(placed_ref[...])
        for i in range(records):
            place_message(placed_ref, layout, frame, into(message_ref, partner(me, i // 4, i % 4, n, 1)), i)
        for c in outs:
            c.wait()

    return kernel


def second_kernel(frame, layout, records, one_message):
    def kernel(depth_ref, energy_ref, vertical_hbm, table_hbm, sums_hbm, mixed_hbm, wave_hbm, place_hbm, *refs):
        *messages, vertical_ref, table_ref, sums_ref, mixed_ref, wave_ref, place_ref, placed_ref, factors_ref, sems = refs
        copies = start_all([(vertical_hbm, vertical_ref), (table_hbm, table_ref), (sums_hbm, sums_ref), (mixed_hbm, mixed_ref),
                            (wave_hbm, wave_ref), (place_hbm, place_ref)], sems)
        me = lax.axis_index("shard")
        n_channels = sums_ref.shape[0]
        half = sums_ref.shape[1] // 2
        copies[0].wait()
        store_factors(factors_ref, vertical_ref, depth_ref[0], n_channels)
        for c in copies[1:4]:
            c.wait()
        odd = dot(sums_ref[:, half:], table_ref[...])
        whole = (layout.tiles - 1) * LANES
        mixed = odd[:, whole:] + dot(sums_ref[:, :half], mixed_ref[...])
        spec = jnp.concatenate([odd[:, :whole].astype(BF), mixed.astype(BF)], axis=1)
        for c in copies[4:]:
            c.wait()
        placed_ref[...] = dot(place_ref[...], lift(spec, factors_ref, 0, wave_ref))
        pieces = split_energy(energy_ref[...] + energy_of(placed_ref[...]))
        for i in range(records):
            store = into(messages[0], partner(me, i // 4, i % 4, records // 4, 1)) if one_message else into(messages[partners(records).index(i)])
            place_message(placed_ref, layout, frame, store, i, pieces)

    return kernel


def source_order(slot_ref, records, block, source):
    size = records * block
    column = lax.broadcasted_iota(jnp.int32, (1, size), 1)
    goal = jnp.zeros((1, size), jnp.int32)
    for i in range(records):
        goal = jnp.where(column // block == i, slot_ref[source(i)], goal)
    goal = goal * block + column % block
    return jnp.where(lax.broadcasted_iota(jnp.int32, (size, size), 0) == goal, 1.0, 0.0).astype(BF)


def filter_gathers(arrived, layout, forward_ref, inverse_ref, response_ref, out_ref, per, block):
    k = response_ref.shape[0]
    records = k // 2
    blank = jnp.zeros((UNIT, LANES), F32)
    units = [a.astype(F32) for a in arrived]
    for b in range(-(-per // block)):
        live = min(block, per - b * block)
        sides = []
        for t in range(layout.tiles):
            pieces = []
            for a in units:
                for u in range(b * block // UNIT, (b + 1) * block // UNIT):
                    at, up = layout.unit(t, u)
                    piece = blank if at is None else a[at * UNIT : (at + 1) * UNIT]
                    pieces.append(pltpu.roll(piece, UNIT - up, 0) if up else piece)
            sides.append(jnp.concatenate(pieces, axis=0).astype(BF))
        part = dot(forward_ref[: live * k, :], join(sides)).reshape(live, k, layout.tiles * LANES)
        part = part * response_ref[...][None]
        part = part.reshape(live * k, layout.tiles * LANES).astype(BF)
        for g in range(0, live, UNIT):
            some = min(UNIT, live - g)
            back = dot(inverse_ref[: some * records, : some * k], part[g * k : (g + some) * k])
            row = (b * block + g) * records
            out_ref[row : row + some * records, :] = back.astype(BF)


def even_kernel(per, block, layout, records, pairwise):
    def kernel(slot_ref, arrived_ref, forward_hbm, inverse_hbm, response_hbm, table_hbm, *refs):
        *own_hbm, out_ref, forward_b_ref = refs[: 3 if pairwise else 2]
        *own_ref, forward_ref, plain_ref, inverse_ref, response_ref, table_ref, filtered_ref, sems = refs[3 if pairwise else 2 :]
        pairs = [(forward_hbm, plain_ref), (inverse_hbm, inverse_ref), (response_hbm, response_ref), (table_hbm, table_ref)]
        copies = start_all(pairs + list(zip(own_hbm, own_ref)), sems)
        me = lax.axis_index("shard")
        n = records // 4
        for c in copies:
            c.wait()
        forward_ref[...] = dot(plain_ref[...], source_order(slot_ref, records, block, lambda i: i)).astype(BF)
        if pairwise:
            turns = partners(records)
            order = source_order(slot_ref, records, block, lambda i: partner(me, turns[i] // 4, turns[i] % 4, n, -1))
            forward_b_ref[...] = dot(plain_ref[...], order).astype(BF)
        else:
            forward_b_ref[...] = forward_ref[...]
        arrived = [arrived_ref[s] for s in range(records)]
        filter_gathers(arrived, layout, forward_ref, inverse_ref, response_ref, filtered_ref, per, block)
        out_ref[...] = dot(filtered_ref[...], table_ref[...])

    return kernel


def last_kernel(per, block, layout, n_traces, records, one_message):
    def kernel(forward_ref, inverse_ref, response_ref, even_table_ref, odd_table_ref, even_ref, *refs):
        *arrived, out_hbm, filtered_ref, out_ref, sems = refs
        arrived = [arrived[0][s] for s in range(records)] if one_message else [a[...] for a in arrived]
        row = lax.broadcasted_iota(jnp.int32, (UNIT, LANES), 0)
        lane = lax.broadcasted_iota(jnp.int32, (UNIT, LANES), 1)
        ends = sum(a[(layout.units - 1) * UNIT :].astype(F32) for a in arrived)
        ends = jnp.where((row == UNIT - 1) & (lane < 3), ends, 0.0)
        energy = jnp.sum(ends, keepdims=True)
        scale = lax.rsqrt(2.0 * FREQ * (energy * (1.0 / (n_traces * FREQ)) + energy_eps))
        filter_gathers(arrived, layout, forward_ref, inverse_ref, response_ref, filtered_ref, per, block)
        half = even_ref.shape[1]
        strip = 256
        copies = []
        for s in range(0, half, strip):
            odd = dot(filtered_ref[...], odd_table_ref[:, s : s + strip])
            even = even_ref[:, s : s + strip] + dot(filtered_ref[:, (layout.tiles - 1) * LANES :], even_table_ref[:, s : s + strip])
            out_ref[:, s : s + strip] = (even + odd) * scale
            out_ref[:, half + s : half + s + strip] = (even - odd) * scale
            pairs = []
            for here in (pl.ds(s, strip), pl.ds(half + s, strip)):
                pairs.append((out_ref.at[:, here], out_hbm.at[:, here]))
            copies += start_all(pairs, sems, len(copies))
        for c in copies:
            c.wait()

    return kernel


def shards(traces, cable_depth, receiver, shot_slot, gather_home):
    records = lax.axis_size("shard")
    n_rec = gather_home.shape[0]
    per = n_rec // records
    n_channels, n_samples = traces.shape
    half = n_samples // 2
    block = 2 * UNIT if records <= 16 else UNIT
    frame = -(-per // UNIT) * UNIT
    even_tiles, odd_tiles, mixed = bin_tiles()
    n_whole = len(even_tiles)
    last_tiles = odd_tiles + [mixed]
    layout = Layout(per, n_whole, False)
    layout_b = Layout(per, n_whole + 1, True)
    wave = wave_table(n_channels)
    wave_t = np.ascontiguousarray(wave.T)
    even_table = time_table(n_samples, even_tiles, 0)
    mixed_table = time_table(n_samples, [mixed], 0)
    odd_table = time_table(n_samples, last_tiles, 1)
    pad_bins = np.zeros((HALF,), np.int64)
    vertical = vertical_table(n_channels, n_samples, even_tiles)
    vertical_b = vertical_table(n_channels, n_samples, last_tiles + [pad_bins])
    pairwise = records <= 16

    smem = pl.BlockSpec(memory_space=pltpu.SMEM)
    vmem = pl.BlockSpec(memory_space=pltpu.VMEM)
    hbm = pl.BlockSpec(memory_space=pltpu.HBM)
    alone = pltpu.CompilerParams(vmem_limit_bytes=ALL_VMEM)
    shared = pltpu.CompilerParams(vmem_limit_bytes=PART_VMEM)

    def scratch(array):
        return pltpu.VMEM(array.shape, array.dtype)

    message_a, sums, place, energy = pl.pallas_call(
        front_kernel(per, frame, layout, records),
        out_shape=(
            jax.ShapeDtypeStruct((records, layout.units * UNIT, LANES), BF),
            jax.ShapeDtypeStruct((n_channels, n_samples), BF),
            jax.ShapeDtypeStruct((records * frame, wave.shape[0]), BF),
            jax.ShapeDtypeStruct((1, LANES), F32),
        ),
        in_specs=[smem, vmem, vmem] + [hbm] * 5,
        out_specs=(vmem, hbm, hbm, vmem),
        scratch_shapes=[
            scratch(vertical),
            scratch(wave_t),
            scratch(traces),
            scratch(even_table),
            scratch(wave),
            pltpu.VMEM((n_channels, n_samples), BF),
            pltpu.VMEM((records * frame, wave.shape[0]), BF),
            pltpu.VMEM((records * frame, n_whole * LANES), F32),
            pltpu.VMEM((2, n_whole, wave.shape[0] // 2, LANES), F32),
            pltpu.SemaphoreType.DMA((9,)),
        ],
        compiler_params=alone,
        name="front",
    )(cable_depth, receiver, gather_home, vertical, wave_t, traces, even_table, wave)
    arrived_a = lax.all_to_all(message_a, "shard", split_axis=0, concat_axis=0, tiled=True)

    shape_b = (layout_b.units * UNIT, LANES)
    if pairwise:
        shapes_b = tuple(jax.ShapeDtypeStruct(shape_b, BF) for _ in range(records))
    else:
        shapes_b = (jax.ShapeDtypeStruct((records, *shape_b), BF),)
    messages = pl.pallas_call(
        second_kernel(frame, layout_b, records, not pairwise),
        out_shape=shapes_b,
        in_specs=[smem, vmem] + [hbm] * 6,
        out_specs=(vmem,) * len(shapes_b),
        scratch_shapes=[
            scratch(vertical_b),
            scratch(odd_table),
            scratch(sums),
            scratch(mixed_table),
            scratch(wave),
            scratch(place),
            pltpu.VMEM((records * frame, (n_whole + 1) * LANES), F32),
            pltpu.VMEM((2, n_whole + 1, wave.shape[0] // 2, LANES), F32),
            pltpu.SemaphoreType.DMA((6,)),
        ],
        compiler_params=alone,
        name="second",
    )(cable_depth, energy, vertical_b, odd_table, sums, mixed_table, wave, place)
    if pairwise:
        n = records // 4
        arrived_b = list(messages)
        for i, turn in enumerate(partners(records)):
            if i:
                route = [(s, partner(s, turn // 4, turn % 4, n, 1)) for s in range(records)]
                arrived_b[i] = lax.ppermute(messages[i], "shard", route)
    else:
        arrived_b = [lax.all_to_all(messages[0], "shard", split_axis=0, concat_axis=0, tiled=True)]

    forward = shot_forward(records, block)
    inverse = shot_inverse(records)
    response = response_table(records, n_samples, even_tiles)
    even_inverse = np.ascontiguousarray(even_table.T)
    own = arrived_b[:1] if pairwise else []
    even, forward_b, *own = pl.pallas_call(
        even_kernel(per, block, layout, records, pairwise),
        out_shape=(pltpu.VMEM((per * records, half), F32), scratch(forward), *map(scratch, own)),
        in_specs=[smem, vmem] + [hbm] * (4 + len(own)),
        out_specs=(vmem,) * (2 + len(own)),
        scratch_shapes=[
            scratch(forward),
            scratch(forward),
            scratch(inverse),
            scratch(response),
            scratch(even_inverse),
            pltpu.VMEM((per * records, n_whole * LANES), BF),
            pltpu.SemaphoreType.DMA((5,)),
        ],
        compiler_params=shared,
        name="even",
    )(shot_slot, arrived_a, forward, inverse, response, even_inverse, *own)
    arrived_b[: len(own)] = own
    out = pl.pallas_call(
        last_kernel(per, block, layout_b, n_channels * records, records, not pairwise),
        out_shape=jax.ShapeDtypeStruct((per * records, n_samples), F32),
        in_specs=[vmem] * (6 + len(arrived_b)),
        out_specs=hbm,
        scratch_shapes=[
            pltpu.VMEM((per * records, (n_whole + 1) * LANES), BF),
            pltpu.VMEM((per * records, n_samples), F32),
            pltpu.SemaphoreType.DMA((2 * (half // 256),)),
        ],
        compiler_params=shared,
        name="last",
    )(forward_b, inverse, response_table(records, n_samples, last_tiles), np.ascontiguousarray(mixed_table.T),
      np.ascontiguousarray(odd_table.T), even, *arrived_b)
    return out.reshape(per, records, n_samples)


def solution(mesh):
    in_specs = (
        P(("groups", "shard"), None),
        P(("groups", "shard")),
        P(("groups", "shard")),
        P("groups"),
        P("groups"),
    )
    out_specs = P(("groups", "shard"), None, None)
    return jax.shard_map(shards, mesh=mesh, in_specs=in_specs, out_specs=out_specs, check_vma=False)
```

```python
import math

import jax
import jax.numpy as jnp
import ml_dtypes
import numpy as np
from jax import lax
from jax.experimental import pallas as pl
from jax.experimental.pallas import tpu as pltpu
from jax.sharding import PartitionSpec as P


FREQ = 576

sample_step = 0.002
water_speed = 1500.0
channel_spacing = 12.5
shot_spacing = 25.0
surface_reflect = 0.9
ghost_floor = 0.1
reject_speed = 1500.0
low_floor = 4.0 * math.pi
energy_eps = 1e-06

BF = jnp.bfloat16
F32 = jnp.float32
LANES = 128
HALF = 64
UNIT = 8
ALL_VMEM = 60 << 20
MOST_VMEM = 53 << 20
FRONT_VMEM = 52 << 20
PART_VMEM = 36 << 20


def to_bf16(table):
    return np.asarray(table, np.float32).astype(ml_dtypes.bfloat16)


def bin_tiles():
    even = np.arange(0, FREQ, 2)
    odd = np.arange(1, FREQ, 2)
    whole = len(even) // HALF
    left = len(even) - whole * HALF
    assert 2 * left == HALF and len(odd) == len(even)
    even_tiles = [even[j * HALF : (j + 1) * HALF] for j in range(whole)]
    odd_tiles = [odd[left + j * HALF : left + (j + 1) * HALF] for j in range(whole)]
    mixed = np.concatenate([even[whole * HALF :], odd[:left]])
    return even_tiles, odd_tiles, mixed


def time_table(n_samples, tiles, parity):
    samples = np.arange(n_samples // 2, dtype=np.int64)
    parts = []
    for bins in tiles:
        angle = (samples[:, None] * bins[None, :] % n_samples) * (2.0 * np.pi / n_samples)
        keep = (bins % 2 == parity).astype(np.float64)[None, :]
        parts += [np.cos(angle) * keep, -np.sin(angle) * keep]
    return to_bf16(np.concatenate(parts, axis=1))


def wave_rows(n_channels):
    return -(-(n_channels // 2 + 1) // 16) * 16


def wave_table(n_channels):
    rows = wave_rows(n_channels)
    k = np.arange(rows, dtype=np.int64)
    c = np.arange(n_channels, dtype=np.int64)
    angle = (k[:, None] * c[None, :] % n_channels) * (2.0 * np.pi / n_channels)
    live = (k <= n_channels // 2)[:, None]
    inner = ((k > 0) & (2 * k < n_channels))[:, None]
    return to_bf16(np.concatenate([np.cos(angle) * live, np.sin(angle) * inner], axis=0))


def vertical_table(n_channels, n_samples, tiles):
    rows = wave_rows(n_channels)
    k = np.minimum(np.arange(rows), n_channels // 2).astype(np.float64)
    kx = 2.0 * np.pi * k / (n_channels * channel_spacing)
    bins = np.concatenate(tiles).astype(np.float64)
    slow = 2.0 * np.pi * bins / (n_samples * sample_step) / water_speed
    return (2.0 * np.sqrt(np.maximum(slow[None, :] ** 2 - kx[:, None] ** 2, 0.0))).astype(np.float32)


def shot_basis(records):
    k = np.concatenate([np.arange(records + 1), np.arange(1, records)])
    p = np.arange(records)
    angle = (k[:, None] * p[None, :] % (2 * records)) * (np.pi / records)
    is_sin = (np.arange(2 * records) > records)[:, None]
    return np.where(is_sin, np.sin(angle), np.cos(angle)), k


def shot_forward(records, block):
    basis, _ = shot_basis(records)
    full = np.einsum("kp,gh->gkph", basis, np.eye(block))
    return to_bf16(full.reshape(block * 2 * records, records * block))


def shot_inverse(records):
    basis, _ = shot_basis(records)
    full = np.einsum("kp,gh->gphk", basis, np.eye(UNIT))
    return to_bf16(full.reshape(UNIT * records, UNIT * 2 * records))


def response_table(records, n_samples, tiles):
    _, k = shot_basis(records)
    single = (k == 0) | (k == records)
    parts = []
    for bins in tiles:
        angular = 2.0 * np.pi * bins.astype(np.float64) / (n_samples * sample_step)
        shot_number = 2.0 * np.pi * k / (2 * records * shot_spacing)
        ratio = reject_speed * shot_number[:, None] / (angular[None, :] + low_floor)
        value = 1.0 / (1.0 + ratio**4) / (2.0 * records)
        value = value * np.where(single, 1.0, 2.0)[:, None] * np.where(bins == 0, 1.0, 2.0)[None, :]
        parts += [value, value]
    return np.concatenate(parts, axis=1).astype(np.float32)


def sin_cos(angle):
    turns = jnp.floor(angle * (2.0 / math.pi) + 0.5)
    rest = ((angle - turns * 1.5703125) - turns * 4.837512969970703125e-4) - turns * 7.54978995489188216e-8
    sq = rest * rest
    sine = ((-1.9515295891e-4 * sq + 8.3321608736e-3) * sq - 1.6666654611e-1) * sq * rest + rest
    cosine = ((2.443315711809948e-5 * sq - 1.388731625493765e-3) * sq + 4.166664568298827e-2) * sq * sq - 0.5 * sq + 1.0
    quarter = turns.astype(jnp.int32)
    odd = (quarter & 1) == 1
    sin_out = jnp.where(odd, cosine, sine)
    cos_out = jnp.where(odd, sine, cosine)
    sin_out = jnp.where((quarter & 2) == 2, -sin_out, sin_out)
    cos_out = jnp.where(((quarter + 1) & 2) == 2, -cos_out, cos_out)
    return sin_out, cos_out


def gains(vertical, depth, weight):
    sine, cosine = sin_cos(vertical * depth)
    denominator = 1.0 - 2.0 * surface_reflect * cosine + surface_reflect * surface_reflect + ghost_floor
    scale = weight / denominator
    return (1.0 - surface_reflect * cosine) * scale, -surface_reflect * sine * scale


def tile_gains(gain_re, gain_im, second):
    lane = lax.broadcasted_iota(jnp.int32, gain_re.shape, 1)
    low = lane < HALF
    re_other = pltpu.roll(gain_re, HALF, 1)
    im_other = pltpu.roll(gain_im, HALF, 1)
    if second:
        return jnp.where(low, re_other, gain_re), jnp.where(low, -im_other, gain_im)
    return jnp.where(low, gain_re, re_other), jnp.where(low, -gain_im, im_other)


def dot(a, b):
    return jnp.dot(a, b, preferred_element_type=F32)


def lift(spec, factors_ref, first, wave_ref):
    rows = wave_ref.shape[0] // 2
    plain = dot(wave_ref[...], spec)
    lifted = []
    for t in range(spec.shape[1] // LANES):
        same = factors_ref[0, first + t]
        swapped = factors_ref[1, first + t]
        both = []
        for h in range(2):
            part = plain[h * rows : (h + 1) * rows, t * LANES : (t + 1) * LANES]
            both.append((part * same + pltpu.roll(part, HALF, 1) * swapped).astype(BF))
        lifted.append(jnp.concatenate(both, axis=0))
    return join(lifted)


def store_factors(factors_ref, vertical_ref, depth, n_channels):
    tiles = factors_ref.shape[1]
    row = lax.broadcasted_iota(jnp.int32, (vertical_ref.shape[0], LANES), 0)
    single = (row == 0) | (row * 2 == n_channels)
    weight = jnp.where(single, 1.0 / n_channels, 2.0 / n_channels)
    for t in range(0, tiles, 2):
        gain_re, gain_im = gains(vertical_ref[:, t * HALF : (t + 2) * HALF], depth, weight)
        for h in range(min(2, tiles - t)):
            factors_ref[0, t + h], factors_ref[1, t + h] = tile_gains(gain_re, gain_im, h == 1)


def join(parts):
    return parts[0] if len(parts) == 1 else jnp.concatenate(parts, axis=1)


def energy_of(cleaned):
    total = jnp.sum(cleaned * cleaned, axis=0, keepdims=True)
    return sum(total[:, t * LANES : (t + 1) * LANES] for t in range(cleaned.shape[1] // LANES))


class Layout:
    def __init__(self, per, tiles, spare):
        self.whole = per // UNIT
        self.left = per % UNIT
        self.tiles = tiles
        self.shared = UNIT // self.left if self.left else 1
        rows = tiles * self.left
        self.left_units = -(-tiles // self.shared) if self.left else 0
        if spare and rows - (self.left_units - 1) * self.shared * self.left == UNIT or spare and not self.left_units:
            self.left_units += 1
        self.units = self.whole * tiles + self.left_units

    def unit(self, tile, u):
        if u < self.whole:
            return tile * self.whole + u, 0
        if u == self.whole and self.left:
            return self.whole * self.tiles + tile // self.shared, tile % self.shared * self.left
        return None, 0


def partner(me, dz, lo, n, sign):
    return (me // 4 + (dz if sign > 0 else n - dz)) % n * 4 + ((me % 4) ^ lo)


def chips(records):
    n = records // 4
    far = sorted(range(1, n), key=lambda d: -min(d, n - d))
    return [2 * dz + dx for dz in far for dx in range(2)] + [1]


def place_message(placed, layout, frame, store, i, energy=None):
    mine = placed[i * frame : (i + 1) * frame]
    parts = [mine[: layout.whole * UNIT, t * LANES : (t + 1) * LANES] for t in range(layout.tiles)] if layout.whole else []
    left = [jnp.zeros((UNIT, LANES), F32) for _ in range(layout.left_units)]
    if layout.left:
        row = lax.broadcasted_iota(jnp.int32, (UNIT, LANES), 0)
        for t in range(layout.tiles):
            unit = mine[layout.whole * UNIT : (layout.whole + 1) * UNIT, t * LANES : (t + 1) * LANES]
            shift = t % layout.shared * layout.left
            unit = jnp.where(row < layout.left, unit, 0.0)
            left[t // layout.shared] += pltpu.roll(unit, shift, 0) if shift else unit
    if energy is not None:
        row = lax.broadcasted_iota(jnp.int32, (UNIT, LANES), 0)
        left[-1] = jnp.where(row == UNIT - 1, energy, left[-1])
    store(jnp.concatenate(parts + left, axis=0).astype(BF))


def split_energy(energy):
    total = jnp.sum(energy, axis=1, keepdims=True)
    high = total.astype(BF).astype(F32)
    middle = (total - high).astype(BF).astype(F32)
    low = total - high - middle
    lane = lax.broadcasted_iota(jnp.int32, (1, LANES), 1)
    return jnp.where(lane == 0, high, jnp.where(lane == 1, middle, jnp.where(lane == 2, low, 0.0)))


def into(ref, index=None):
    def store(value):
        if index is None:
            ref[...] = value
        else:
            ref[index] = value

    return store


def start_all(pairs, sems, first=0):
    copies = [pltpu.make_async_copy(a, b, sems.at[first + i]) for i, (a, b) in enumerate(pairs)]
    for c in copies:
        c.start()
    return copies


def front_kernel(per, frame, layout, records, count):
    def kernel(depth_ref, receiver_ref, home_ref, vertical_hbm, wave_hbm, traces_hbm, table_hbm, mixed_hbm, *refs):
        later_hbm = refs[:2]
        *messages, odd_ref, place_ref, wave_ref, energy_ref = refs[2 : 6 + count]
        later = refs[6 + count : 8 + count]
        vertical_ref, traces_ref, table_ref, mixed_ref, sum_ref, placed_ref, factors_ref, sems = refs[8 + count :]
        me = lax.axis_index("shard")
        n_channels, n_samples = traces_ref.shape
        half = n_samples // 2
        steps = 3
        step = n_channels // steps
        pairs = [(traces_hbm.at[pl.ds(s * step, step), :], traces_ref.at[pl.ds(s * step, step), :]) for s in range(steps)]
        pairs = [(vertical_hbm, vertical_ref), (wave_hbm, wave_ref), *pairs, (table_hbm, table_ref), (mixed_hbm, mixed_ref)]
        copies = start_all(pairs, sems)
        n_rec = home_ref.shape[0]
        home = home_ref[...].reshape(1, n_rec)
        device = jnp.floor((home.astype(F32) + 0.5) * (1.0 / per)).astype(jnp.int32)
        n = records // 4
        turn = (device >> 2) - me // 4
        turn = jnp.where(turn < 0, turn + n, turn)
        home_row = (turn * 4 + ((device & 3) ^ (me % 4))) * frame + (home - device * per)
        both = jnp.concatenate([home_row >> 7, home_row & 127, jnp.zeros((14, n_rec), jnp.int32)], axis=0).astype(F32).astype(BF)
        to_bin = lax.broadcasted_iota(jnp.int32, (n_rec, n_channels), 0) == receiver_ref[...].reshape(1, n_channels)
        target = dot(both, jnp.where(to_bin, 1.0, 0.0).astype(BF))
        target = (target[0:1] * 128.0 + target[1:2]).astype(jnp.int32)
        picked = lax.broadcasted_iota(jnp.int32, (records * frame, n_channels), 0) == target
        picked = jnp.where(picked, 1.0, 0.0).astype(BF)
        copies[0].wait()
        copies[1].wait()
        place_ref[...] = lax.dot_general(picked, wave_ref[...], (((1,), (1,)), ((), ())), preferred_element_type=F32).astype(BF)
        store_factors(factors_ref, vertical_ref, depth_ref[0], n_channels)
        outs = start_all(list(zip(later_hbm, later)), sems, len(copies))
        for s in range(steps):
            copies[2 + s].wait()
            part = pl.ds(s * step, step)
            first = traces_ref[part, :half]
            second = traces_ref[part, half:]
            sum_ref[part, :] = (first + second).astype(BF)
            odd_ref[part, :] = (first - second).astype(BF)
        copies[-2].wait()
        even = dot(sum_ref[...], table_ref[...])
        copies[-1].wait()
        whole = (layout.tiles - 1) * LANES
        mixed = even[:, whole:] + dot(odd_ref[...], mixed_ref[...])
        spec = jnp.concatenate([even[:, :whole].astype(BF), mixed.astype(BF)], axis=1)
        placed_ref[...] = dot(place_ref[...], lift(spec, factors_ref, 0, wave_ref))
        energy_ref[...] = energy_of(placed_ref[...])
        for i in range(records):
            store = into(messages[0], partner(me, i // 4, i % 4, n, 1)) if count == 1 else into(messages[i // 2], i % 2)
            place_message(placed_ref, layout, frame, store, i)
        for c in outs:
            c.wait()

    return kernel


def second_kernel(frame, layout, records):
    def kernel(depth_ref, energy_ref, odd_ref, place_ref, wave_ref, table_ref, vertical_ref, message_ref, placed_ref, factors_ref):
        me = lax.axis_index("shard")
        store_factors(factors_ref, vertical_ref, depth_ref[0], odd_ref.shape[0])
        spec = dot(odd_ref[...], table_ref[...]).astype(BF)
        placed_ref[...] = dot(place_ref[...], lift(spec, factors_ref, 0, wave_ref))
        pieces = split_energy(energy_ref[...] + energy_of(placed_ref[...]))
        for i in range(records):
            store = into(message_ref, partner(me, i // 4, i % 4, records // 4, 1))
            place_message(placed_ref, layout, frame, store, i, pieces)

    return kernel


def source_order(slot_ref, records, block, source):
    size = records * block
    column = lax.broadcasted_iota(jnp.int32, (1, size), 1)
    goal = jnp.zeros((1, size), jnp.int32)
    for i in range(records):
        goal = jnp.where(column // block == i, slot_ref[source(i)], goal)
    goal = goal * block + column % block
    return jnp.where(lax.broadcasted_iota(jnp.int32, (size, size), 0) == goal, 1.0, 0.0).astype(BF)


def filter_gathers(arrived, layout, forward_ref, inverse_ref, response_ref, out_ref, per, block):
    k = response_ref.shape[0]
    records = k // 2
    blank = jnp.zeros((UNIT, LANES), F32)
    units = [a.astype(F32) for a in arrived]
    for b in range(-(-per // block)):
        live = min(block, per - b * block)
        sides = []
        for t in range(layout.tiles):
            pieces = []
            for a in units:
                for u in range(b * block // UNIT, (b + 1) * block // UNIT):
                    at, up = layout.unit(t, u)
                    piece = blank if at is None else a[at * UNIT : (at + 1) * UNIT]
                    pieces.append(pltpu.roll(piece, UNIT - up, 0) if up else piece)
            sides.append(jnp.concatenate(pieces, axis=0).astype(BF))
        part = dot(forward_ref[: live * k, :], join(sides)).reshape(live, k, layout.tiles * LANES)
        part = part * response_ref[...][None]
        part = part.reshape(live * k, layout.tiles * LANES).astype(BF)
        for g in range(0, live, UNIT):
            some = min(UNIT, live - g)
            back = dot(inverse_ref[: some * records, : some * k], part[g * k : (g + some) * k])
            row = (b * block + g) * records
            out_ref[row : row + some * records, : layout.tiles * LANES] = back.astype(BF)


def repack_kernel(n):
    def kernel(*refs):
        for chip in range(n):
            refs[n][chip] = refs[chip][1]

    return kernel


def even_kernel(per, block, layout, records, n_sources):
    def kernel(slot_ref, forward_hbm, inverse_hbm, response_hbm, table_hbm, *refs):
        sources = refs[:n_sources]
        (out_hbm, forward_b_hbm, mixed_hbm, out_ref, forward_b_ref, forward_ref, plain_ref, inverse_ref, response_ref, table_ref,
         filtered_ref, sems) = refs[n_sources:]
        me = lax.axis_index("shard")
        n = records // 4
        arrived = []
        for i in range(records):
            if n_sources == 1:
                arrived.append(sources[0][i])
            elif i % 2:
                arrived.append(sources[-1][i // 2])
            else:
                arrived.append(sources[i // 2][0])
        pairs = [(forward_hbm, plain_ref), (inverse_hbm, inverse_ref), (response_hbm, response_ref), (table_hbm, table_ref)]
        copies = start_all(pairs, sems)
        copies[0].wait()
        forward_b_ref[...] = dot(plain_ref[...], source_order(slot_ref, records, block, lambda i: i)).astype(BF)
        if n_sources == 1:
            forward_ref[...] = forward_b_ref[...]
        else:
            order = source_order(slot_ref, records, block, lambda i: partner(me, i // 4, i % 4, n, -1))
            forward_ref[...] = dot(plain_ref[...], order).astype(BF)
        for c in copies[1:]:
            c.wait()
        filter_gathers(arrived, layout, forward_ref, inverse_ref, response_ref, filtered_ref, per, block)
        mixed = filtered_ref.at[:, pl.ds((layout.tiles - 1) * LANES, LANES)]
        outs = start_all([(forward_b_ref, forward_b_hbm), (mixed, mixed_hbm)], sems, 4)
        out_ref[...] = dot(filtered_ref[...], table_ref[...])
        for c in outs + start_all([(out_ref, out_hbm)], sems, 6):
            c.wait()

    return kernel


def last_kernel(per, block, layout, n_traces, records):
    def kernel(arrived_hbm, forward_hbm, inverse_hbm, response_hbm, mixed_hbm, odd_table_hbm, even_hbm,
               out_hbm, arrived_ref, forward_ref, inverse_ref, response_ref, odd_table_ref, even_ref, filtered_ref, out_ref, sems):
        half = even_ref.shape[1]
        strip = 256
        cuts = [pl.ds(s, strip) for s in range(0, half, strip)]
        mixed = filtered_ref.at[:, pl.ds(layout.tiles * LANES, LANES)]
        first = [(arrived_hbm, arrived_ref), (forward_hbm, forward_ref), (inverse_hbm, inverse_ref), (response_hbm, response_ref)]
        fetch = start_all(first + [(odd_table_hbm, odd_table_ref), (mixed_hbm, mixed)], sems)
        fetch += start_all([(even_hbm.at[:, c], even_ref.at[:, c]) for c in cuts], sems, len(fetch))
        for c in fetch[:4]:
            c.wait()
        arrived = [arrived_ref[s] for s in range(records)]
        row = lax.broadcasted_iota(jnp.int32, (UNIT, LANES), 0)
        lane = lax.broadcasted_iota(jnp.int32, (UNIT, LANES), 1)
        ends = sum(a[(layout.units - 1) * UNIT :].astype(F32) for a in arrived)
        ends = jnp.where((row == UNIT - 1) & (lane < 3), ends, 0.0)
        energy = jnp.sum(ends, keepdims=True)
        scale = lax.rsqrt(2.0 * FREQ * (energy * (1.0 / (n_traces * FREQ)) + energy_eps))
        filter_gathers(arrived, layout, forward_ref, inverse_ref, response_ref, filtered_ref, per, block)
        for c in fetch[4:6]:
            c.wait()
        copies = []
        for s in range(0, half, strip):
            fetch[6 + s // strip].wait()
            odd = dot(filtered_ref[...], odd_table_ref[:, s : s + strip])
            even = even_ref[:, s : s + strip]
            out_ref[:, s : s + strip] = (even + odd) * scale
            out_ref[:, half + s : half + s + strip] = (even - odd) * scale
            pairs = []
            for here in (pl.ds(s, strip), pl.ds(half + s, strip)):
                pairs.append((out_ref.at[:, here], out_hbm.at[:, here]))
            copies += start_all(pairs, sems, len(fetch) + len(copies))
        for c in copies:
            c.wait()

    return kernel


def shards(traces, cable_depth, receiver, shot_slot, gather_home):
    records = lax.axis_size("shard")
    n_rec = gather_home.shape[0]
    per = n_rec // records
    n_channels, n_samples = traces.shape
    half = n_samples // 2
    block = 2 * UNIT if records <= 16 else UNIT
    frame = -(-per // UNIT) * UNIT
    even_tiles, odd_tiles, mixed = bin_tiles()
    n_whole = len(even_tiles)
    layout = Layout(per, n_whole + 1, False)
    layout_b = Layout(per, n_whole, True)
    wave = wave_table(n_channels)
    even_table = time_table(n_samples, even_tiles + [mixed], 0)
    odd_table = time_table(n_samples, odd_tiles + [mixed], 1)
    mixed_odd = np.ascontiguousarray(odd_table[:, n_whole * LANES :])
    odd_whole = np.ascontiguousarray(odd_table[:, : n_whole * LANES])
    pad_bins = np.zeros((HALF,), np.int64)
    vertical = vertical_table(n_channels, n_samples, even_tiles + [mixed, pad_bins])
    vertical_b = vertical_table(n_channels, n_samples, odd_tiles)
    pairwise = records <= 16

    smem = pl.BlockSpec(memory_space=pltpu.SMEM)
    vmem = pl.BlockSpec(memory_space=pltpu.VMEM)
    hbm = pl.BlockSpec(memory_space=pltpu.HBM)
    alone = pltpu.CompilerParams(vmem_limit_bytes=ALL_VMEM)
    most = pltpu.CompilerParams(vmem_limit_bytes=MOST_VMEM)
    shared = pltpu.CompilerParams(vmem_limit_bytes=PART_VMEM)

    def scratch(array):
        return pltpu.VMEM(array.shape, array.dtype)

    n = records // 4
    planes = records // 2 if pairwise else 1
    *sources, odd, place, wave_kept, energy, odd_kept, vertical_kept = pl.pallas_call(
        front_kernel(per, frame, layout, records, planes),
        out_shape=(
            *(jax.ShapeDtypeStruct((records // planes, layout.units * UNIT, LANES), BF) for _ in range(planes)),
            pltpu.VMEM((n_channels, half), BF),
            pltpu.VMEM((records * frame, wave.shape[0]), BF),
            scratch(wave),
            pltpu.VMEM((1, LANES), F32),
            scratch(odd_whole),
            scratch(vertical_b),
        ),
        in_specs=[smem, vmem, vmem] + [hbm] * 7,
        out_specs=(vmem,) * (6 + planes),
        scratch_shapes=[
            scratch(vertical),
            scratch(traces),
            scratch(even_table),
            scratch(mixed_odd),
            pltpu.VMEM((n_channels, half), BF),
            pltpu.VMEM((records * frame, (n_whole + 1) * LANES), F32),
            pltpu.VMEM((2, n_whole + 1, wave.shape[0] // 2, LANES), F32),
            pltpu.SemaphoreType.DMA((10,)),
        ],
        compiler_params=pltpu.CompilerParams(vmem_limit_bytes=FRONT_VMEM),
        name="front",
    )(cable_depth, receiver, gather_home, vertical, wave, traces, even_table, mixed_odd, odd_whole, vertical_b)
    if pairwise:
        for chip in chips(records):
            route = [(s, partner(s, chip // 2, chip % 2 * 2, n, 1)) for s in range(records)]
            sources[chip] = lax.ppermute(sources[chip], "shard", route)
    else:
        sources = [lax.all_to_all(sources[0], "shard", split_axis=0, concat_axis=0, tiled=True)]

    second = pl.pallas_call(
        second_kernel(frame, layout_b, records),
        out_shape=jax.ShapeDtypeStruct((records, layout_b.units * UNIT, LANES), BF),
        in_specs=[smem] + [vmem] * 6,
        out_specs=vmem,
        scratch_shapes=[
            pltpu.VMEM((records * frame, n_whole * LANES), F32),
            pltpu.VMEM((2, n_whole, wave.shape[0] // 2, LANES), F32),
        ],
        compiler_params=shared,
        name="second",
    )
    message_b = second(cable_depth, energy, odd, place, wave_kept, odd_kept, vertical_kept)
    arrived_b = lax.all_to_all(message_b, "shard", split_axis=0, concat_axis=0, tiled=True)

    if pairwise:
        packed = pl.pallas_call(
            repack_kernel(planes),
            out_shape=jax.ShapeDtypeStruct((planes, *sources[0].shape[1:]), BF),
            in_specs=[vmem] * planes,
            out_specs=vmem,
            compiler_params=shared,
            name="repack",
        )(*sources)
        sources.append(lax.ppermute(packed, "shard", [(s, s ^ 1) for s in range(records)]))

    forward = shot_forward(records, block)
    inverse = shot_inverse(records)
    response = response_table(records, n_samples, even_tiles + [mixed])
    even_inverse = np.ascontiguousarray(even_table.T)
    even, forward_b, mixed_part = pl.pallas_call(
        even_kernel(per, block, layout, records, len(sources)),
        out_shape=(
            jax.ShapeDtypeStruct((per * records, half), F32),
            jax.ShapeDtypeStruct(forward.shape, BF),
            jax.ShapeDtypeStruct((per * records, LANES), BF),
        ),
        in_specs=[smem] + [hbm] * 4 + [vmem] * len(sources),
        out_specs=(hbm,) * 3,
        scratch_shapes=[
            pltpu.VMEM((per * records, half), F32),
            scratch(forward),
            scratch(forward),
            scratch(forward),
            scratch(inverse),
            scratch(response),
            scratch(even_inverse),
            pltpu.VMEM((per * records, (n_whole + 1) * LANES), BF),
            pltpu.SemaphoreType.DMA((7,)),
        ],
        compiler_params=shared,
        name="even",
    )(shot_slot, forward, inverse, response, even_inverse, *sources)
    out = pl.pallas_call(
        last_kernel(per, block, layout_b, n_channels * records, records),
        out_shape=jax.ShapeDtypeStruct((per * records, n_samples), F32),
        in_specs=[hbm] * 7,
        out_specs=hbm,
        scratch_shapes=[
            scratch(arrived_b),
            scratch(forward),
            scratch(inverse),
            pltpu.VMEM((2 * records, n_whole * LANES), F32),
            scratch(odd_table.T),
            pltpu.VMEM((per * records, half), F32),
            pltpu.VMEM((per * records, (n_whole + 1) * LANES), BF),
            pltpu.VMEM((per * records, n_samples), F32),
            pltpu.SemaphoreType.DMA((6 + 3 * (half // 256),)),
        ],
        compiler_params=most,
        name="last",
    )(arrived_b, forward_b, inverse, response_table(records, n_samples, odd_tiles), mixed_part, np.ascontiguousarray(odd_table.T), even)
    return out.reshape(per, records, n_samples)


def solution(mesh):
    in_specs = (
        P(("groups", "shard"), None),
        P(("groups", "shard")),
        P(("groups", "shard")),
        P("groups"),
        P("groups"),
    )
    out_specs = P(("groups", "shard"), None, None)
    return jax.shard_map(shards, mesh=mesh, in_specs=in_specs, out_specs=out_specs, check_vma=False)
```

```python
import math

import jax
import jax.numpy as jnp
import ml_dtypes
import numpy as np
from jax import lax
from jax.experimental import pallas as pl
from jax.experimental.pallas import tpu as pltpu
from jax.sharding import PartitionSpec as P


FREQ = 576

sample_step = 0.002
water_speed = 1500.0
channel_spacing = 12.5
shot_spacing = 25.0
surface_reflect = 0.9
ghost_floor = 0.1
reject_speed = 1500.0
low_floor = 4.0 * math.pi
energy_eps = 1e-06

BF = jnp.bfloat16
F32 = jnp.float32
LANES = 128
HALF = 64
UNIT = 8
STRIP = 512
ALL_VMEM = 60 << 20
MOST_VMEM = 53 << 20
FRONT_VMEM = 52 << 20
PART_VMEM = 36 << 20


def to_bf16(table):
    return np.asarray(table, np.float32).astype(ml_dtypes.bfloat16)


def bin_tiles():
    even = np.arange(0, FREQ, 2)
    odd = np.arange(1, FREQ, 2)
    whole = len(even) // HALF
    left = len(even) - whole * HALF
    assert 2 * left == HALF and len(odd) == len(even)
    even_tiles = [even[j * HALF : (j + 1) * HALF] for j in range(whole)]
    odd_tiles = [odd[left + j * HALF : left + (j + 1) * HALF] for j in range(whole)]
    mixed = np.concatenate([even[whole * HALF :], odd[:left]])
    return even_tiles, odd_tiles, mixed


def time_table(n_samples, tiles, parity):
    samples = np.arange(n_samples // 2, dtype=np.int64)
    parts = []
    for bins in tiles:
        angle = (samples[:, None] * bins[None, :] % n_samples) * (2.0 * np.pi / n_samples)
        keep = (bins % 2 == parity).astype(np.float64)[None, :]
        parts += [np.cos(angle) * keep, -np.sin(angle) * keep]
    return to_bf16(np.concatenate(parts, axis=1))


def wave_rows(n_channels):
    return -(-(n_channels // 2 + 1) // 16) * 16


def wave_table(n_channels):
    rows = wave_rows(n_channels)
    k = np.arange(rows, dtype=np.int64)
    c = np.arange(n_channels, dtype=np.int64)
    angle = (k[:, None] * c[None, :] % n_channels) * (2.0 * np.pi / n_channels)
    live = (k <= n_channels // 2)[:, None]
    inner = ((k > 0) & (2 * k < n_channels))[:, None]
    return to_bf16(np.concatenate([np.cos(angle) * live, np.sin(angle) * inner], axis=0))


def vertical_table(n_channels, n_samples, tiles):
    rows = wave_rows(n_channels)
    k = np.minimum(np.arange(rows), n_channels // 2).astype(np.float64)
    kx = 2.0 * np.pi * k / (n_channels * channel_spacing)
    bins = np.concatenate(tiles).astype(np.float64)
    slow = 2.0 * np.pi * bins / (n_samples * sample_step) / water_speed
    return np.sqrt(np.maximum(slow[None, :] ** 2 - kx[:, None] ** 2, 0.0)).astype(np.float32)


def shot_basis(records):
    k = np.concatenate([np.arange(records + 1), np.arange(1, records)])
    p = np.arange(records)
    angle = (k[:, None] * p[None, :] % (2 * records)) * (np.pi / records)
    is_sin = (np.arange(2 * records) > records)[:, None]
    return np.where(is_sin, np.sin(angle), np.cos(angle)), k


def shot_forward(records, block):
    basis, _ = shot_basis(records)
    full = np.einsum("kp,gh->gkph", basis, np.eye(block))
    return to_bf16(full.reshape(block * 2 * records, records * block))


def shot_inverse(records):
    basis, _ = shot_basis(records)
    full = np.einsum("kp,gh->gphk", basis, np.eye(UNIT))
    return to_bf16(full.reshape(UNIT * records, UNIT * 2 * records))


def response_table(records, n_samples, tiles):
    _, k = shot_basis(records)
    single = (k == 0) | (k == records)
    parts = []
    for bins in tiles:
        angular = 2.0 * np.pi * bins.astype(np.float64) / (n_samples * sample_step)
        shot_number = 2.0 * np.pi * k / (2 * records * shot_spacing)
        ratio = reject_speed * shot_number[:, None] / (angular[None, :] + low_floor)
        value = 1.0 / (1.0 + ratio**4) / (2.0 * records)
        value = value * np.where(single, 1.0, 2.0)[:, None] * np.where(bins == 0, 1.0, 2.0)[None, :]
        parts += [value, value]
    return np.concatenate(parts, axis=1).astype(np.float32)


def sin_cos(angle):
    turns = jnp.floor(angle * (1.0 / math.pi) + 0.5)
    rest = ((angle - turns * 3.140625) - turns * 9.67502593994140625e-4) - turns * 1.509957990978376432e-7
    sq = rest * rest
    sine = -2.3889859e-8 * sq + 2.7525562e-6
    sine = sine * sq - 1.9840874e-4
    sine = sine * sq + 8.3333310e-3
    sine = sine * sq - 1.6666667e-1
    sine = sine * sq * rest + rest
    cosine = -2.605e-7 * sq + 2.47609e-5
    cosine = cosine * sq - 1.3888397e-3
    cosine = cosine * sq + 4.16666418e-2
    cosine = cosine * sq - 0.4999999963
    cosine = cosine * sq + 1.0
    return sine, cosine


def gains(vertical, depth, weight):
    sine, cosine = sin_cos(vertical * depth)
    double = 2.0 * sine
    less = sine * double
    top = 1.0 - surface_reflect
    bottom = 1.0 - 2.0 * surface_reflect + surface_reflect * surface_reflect + ghost_floor
    scale = weight / (bottom + 2.0 * surface_reflect * less)
    return (top + surface_reflect * less) * scale, (-surface_reflect * double) * cosine * scale


def tile_gains(gain_re, gain_im, second):
    lane = lax.broadcasted_iota(jnp.int32, gain_re.shape, 1)
    low = lane < HALF
    re_other = pltpu.roll(gain_re, HALF, 1)
    im_other = pltpu.roll(gain_im, HALF, 1)
    if second:
        return jnp.where(low, re_other, gain_re), jnp.where(low, -im_other, gain_im)
    return jnp.where(low, gain_re, re_other), jnp.where(low, -gain_im, im_other)


def dot(a, b):
    return jnp.dot(a, b, preferred_element_type=F32)


def lift(spec, factors_ref, first, wave_ref):
    rows = wave_ref.shape[0] // 2
    plain = dot(wave_ref[...], spec)
    lifted = []
    for t in range(spec.shape[1] // LANES):
        same = factors_ref[0, first + t]
        swapped = factors_ref[1, first + t]
        both = []
        for h in range(2):
            part = plain[h * rows : (h + 1) * rows, t * LANES : (t + 1) * LANES]
            both.append((part * same + pltpu.roll(part, HALF, 1) * swapped).astype(BF))
        lifted.append(jnp.concatenate(both, axis=0))
    return join(lifted)


def store_factors(factors_ref, vertical_ref, depth, n_channels, first=None):
    tiles = factors_ref.shape[1]
    row = lax.broadcasted_iota(jnp.int32, (vertical_ref.shape[0], LANES), 0)
    single = (row == 0) | (row * 2 == n_channels)
    weight = jnp.where(single, 1.0 / n_channels, 2.0 / n_channels)
    for t in range(0, tiles, 2) if first is None else (first,):
        gain_re, gain_im = gains(vertical_ref[:, t * HALF : (t + 2) * HALF], depth, weight)
        for h in range(min(2, tiles - t)):
            factors_ref[0, t + h], factors_ref[1, t + h] = tile_gains(gain_re, gain_im, h == 1)


def join(parts):
    return parts[0] if len(parts) == 1 else jnp.concatenate(parts, axis=1)


def energy_of(cleaned):
    total = jnp.sum(cleaned * cleaned, axis=0, keepdims=True)
    return sum(total[:, t * LANES : (t + 1) * LANES] for t in range(cleaned.shape[1] // LANES))


class Layout:
    def __init__(self, per, tiles, spare):
        self.whole = per // UNIT
        self.left = per % UNIT
        self.tiles = tiles
        self.shared = UNIT // self.left if self.left else 1
        rows = tiles * self.left
        self.left_units = -(-tiles // self.shared) if self.left else 0
        if spare and rows - (self.left_units - 1) * self.shared * self.left == UNIT or spare and not self.left_units:
            self.left_units += 1
        self.units = self.whole * tiles + self.left_units

    def unit(self, tile, u):
        if u < self.whole:
            return tile * self.whole + u, 0
        if u == self.whole and self.left:
            return self.whole * self.tiles + tile // self.shared, tile % self.shared * self.left
        return None, 0


def partner(me, dz, lo, n, sign):
    return (me // 4 + (dz if sign > 0 else n - dz)) % n * 4 + ((me % 4) ^ lo)


def chips(records):
    n = records // 4
    far = sorted(range(1, n), key=lambda d: min(d, n - d))
    return [2 * dz + dx for dz in far for dx in range(2)] + [1]


def place_message(placed, layout, frame, store, i, energy=None):
    mine = placed[i * frame : (i + 1) * frame]
    parts = [mine[: layout.whole * UNIT, t * LANES : (t + 1) * LANES] for t in range(layout.tiles)] if layout.whole else []
    left = [jnp.zeros((UNIT, LANES), F32) for _ in range(layout.left_units)]
    if layout.left:
        row = lax.broadcasted_iota(jnp.int32, (UNIT, LANES), 0)
        for t in range(layout.tiles):
            unit = mine[layout.whole * UNIT : (layout.whole + 1) * UNIT, t * LANES : (t + 1) * LANES]
            shift = t % layout.shared * layout.left
            unit = jnp.where(row < layout.left, unit, 0.0)
            left[t // layout.shared] += pltpu.roll(unit, shift, 0) if shift else unit
    if energy is not None:
        row = lax.broadcasted_iota(jnp.int32, (UNIT, LANES), 0)
        left[-1] = jnp.where(row == UNIT - 1, energy, left[-1])
    store(jnp.concatenate(parts + left, axis=0).astype(BF))


def split_energy(energy):
    total = jnp.sum(energy, axis=1, keepdims=True)
    high = total.astype(BF).astype(F32)
    middle = (total - high).astype(BF).astype(F32)
    low = total - high - middle
    lane = lax.broadcasted_iota(jnp.int32, (1, LANES), 1)
    return jnp.where(lane == 0, high, jnp.where(lane == 1, middle, jnp.where(lane == 2, low, 0.0)))


def into(ref, index=None):
    def store(value):
        if index is None:
            ref[...] = value
        else:
            ref[index] = value

    return store


def start_all(pairs, sems, first=0):
    copies = [pltpu.make_async_copy(a, b, sems.at[first + i]) for i, (a, b) in enumerate(pairs)]
    for c in copies:
        c.start()
    return copies


def front_kernel(per, frame, layout, records, count):
    def kernel(depth_ref, receiver_ref, home_ref, vertical_hbm, wave_hbm, traces_hbm, table_hbm, mixed_hbm, *refs):
        later_hbm = refs[:2]
        *messages, odd_ref, place_ref, wave_ref, energy_ref = refs[2 : 6 + count]
        later = refs[6 + count : 8 + count]
        vertical_ref, traces_ref, table_ref, mixed_ref, sum_ref, placed_ref, factors_ref, sems = refs[8 + count :]
        me = lax.axis_index("shard")
        n_channels, n_samples = traces_ref.shape
        half = n_samples // 2
        steps = 3
        step = n_channels // steps
        pairs = [(traces_hbm.at[pl.ds(s * step, step), :], traces_ref.at[pl.ds(s * step, step), :]) for s in range(steps)]
        pairs = [(vertical_hbm, vertical_ref), (wave_hbm, wave_ref), *pairs, (table_hbm, table_ref), (mixed_hbm, mixed_ref)]
        copies = start_all(pairs, sems)
        n_rec = home_ref.shape[0]
        home = home_ref[...].reshape(1, n_rec)
        device = jnp.floor((home.astype(F32) + 0.5) * (1.0 / per)).astype(jnp.int32)
        n = records // 4
        turn = (device >> 2) - me // 4
        turn = jnp.where(turn < 0, turn + n, turn)
        home_row = (turn * 4 + ((device & 3) ^ (me % 4))) * frame + (home - device * per)
        both = jnp.concatenate([home_row >> 7, home_row & 127, jnp.zeros((14, n_rec), jnp.int32)], axis=0).astype(F32).astype(BF)
        to_bin = lax.broadcasted_iota(jnp.int32, (n_rec, n_channels), 0) == receiver_ref[...].reshape(1, n_channels)
        target = dot(both, jnp.where(to_bin, 1.0, 0.0).astype(BF))
        target = (target[0:1] * 128.0 + target[1:2]).astype(jnp.int32)
        picked = lax.broadcasted_iota(jnp.int32, (records * frame, n_channels), 0) == target
        picked = jnp.where(picked, 1.0, 0.0).astype(BF)
        copies[0].wait()
        copies[1].wait()
        place_ref[...] = lax.dot_general(picked, wave_ref[...], (((1,), (1,)), ((), ())), preferred_element_type=F32).astype(BF)
        outs = start_all(list(zip(later_hbm, later)), sems, len(copies))
        for s in range(steps):
            copies[2 + s].wait()
            part = pl.ds(s * step, step)
            first = traces_ref[part, :half]
            second = traces_ref[part, half:]
            sum_ref[part, :] = (first + second).astype(BF)
            odd_ref[part, :] = (first - second).astype(BF)
        for c in copies[-2:]:
            c.wait()
        spec = []
        for t in range(0, layout.tiles, 2):
            cols = slice(t * LANES, min(t + 2, layout.tiles) * LANES)
            got = dot(sum_ref[...], table_ref[:, cols])
            if t + 2 > layout.tiles:
                got = got + dot(odd_ref[...], mixed_ref[...])
            spec.append(got.astype(BF))
            store_factors(factors_ref, vertical_ref, depth_ref[0], n_channels, t)
        spec = jnp.concatenate(spec, axis=1)
        placed_ref[...] = dot(place_ref[...], lift(spec, factors_ref, 0, wave_ref))
        energy_ref[...] = energy_of(placed_ref[...])
        for i in range(records):
            store = into(messages[0], partner(me, i // 4, i % 4, n, 1)) if count == 1 else into(messages[i // 2], i % 2)
            place_message(placed_ref, layout, frame, store, i)
        for c in outs:
            c.wait()

    return kernel


def second_kernel(frame, layout, records):
    def kernel(depth_ref, energy_ref, odd_ref, place_ref, wave_ref, table_ref, vertical_ref, message_ref, placed_ref, factors_ref):
        me = lax.axis_index("shard")
        store_factors(factors_ref, vertical_ref, depth_ref[0], odd_ref.shape[0])
        spec = dot(odd_ref[...], table_ref[...]).astype(BF)
        placed_ref[...] = dot(place_ref[...], lift(spec, factors_ref, 0, wave_ref))
        pieces = split_energy(energy_ref[...] + energy_of(placed_ref[...]))
        for i in range(records):
            store = into(message_ref, partner(me, i // 4, i % 4, records // 4, 1))
            place_message(placed_ref, layout, frame, store, i, pieces)

    return kernel


def source_order(slot_ref, records, block, source):
    size = records * block
    column = lax.broadcasted_iota(jnp.int32, (1, size), 1)
    goal = jnp.zeros((1, size), jnp.int32)
    for i in range(records):
        goal = jnp.where(column // block == i, slot_ref[source(i)], goal)
    goal = goal * block + column % block
    return jnp.where(lax.broadcasted_iota(jnp.int32, (size, size), 0) == goal, 1.0, 0.0).astype(BF)


def filter_gathers(arrived, layout, forward_ref, inverse_ref, response_ref, out_ref, per, block, blocks=None):
    k = response_ref.shape[0]
    records = k // 2
    blank = jnp.zeros((UNIT, LANES), F32)
    units = [a.astype(F32) for a in arrived]
    for b in range(-(-per // block)) if blocks is None else blocks:
        live = min(block, per - b * block)
        sides = []
        for t in range(layout.tiles):
            pieces = []
            for a in units:
                for u in range(b * block // UNIT, (b + 1) * block // UNIT):
                    at, up = layout.unit(t, u)
                    piece = blank if at is None else a[at * UNIT : (at + 1) * UNIT]
                    pieces.append(pltpu.roll(piece, UNIT - up, 0) if up else piece)
            sides.append(jnp.concatenate(pieces, axis=0).astype(BF))
        part = dot(forward_ref[: live * k, :], join(sides)).reshape(live, k, layout.tiles * LANES)
        part = part * response_ref[...][None]
        part = part.reshape(live * k, layout.tiles * LANES).astype(BF)
        for g in range(0, live, UNIT):
            some = min(UNIT, live - g)
            back = dot(inverse_ref[: some * records, : some * k], part[g * k : (g + some) * k])
            row = (b * block + g) * records
            out_ref[row : row + some * records, : layout.tiles * LANES] = back.astype(BF)


def repack_kernel(n):
    def kernel(*refs):
        for chip in range(n):
            refs[n][chip] = refs[chip][1]

    return kernel


def even_kernel(per, block, layout, records, n_sources):
    def kernel(slot_ref, forward_hbm, inverse_hbm, response_hbm, table_hbm, *refs):
        sources = refs[:n_sources]
        (out_hbm, forward_b_hbm, mixed_hbm, out_ref, forward_b_ref, forward_ref, plain_ref, inverse_ref, response_ref, table_ref,
         filtered_ref, sems) = refs[n_sources:]
        me = lax.axis_index("shard")
        n = records // 4
        arrived = []
        for i in range(records):
            if n_sources == 1:
                arrived.append(sources[0][i])
            elif i % 2:
                arrived.append(sources[-1][i // 2])
            else:
                arrived.append(sources[i // 2][0])
        pairs = [(forward_hbm, plain_ref), (inverse_hbm, inverse_ref), (response_hbm, response_ref), (table_hbm, table_ref)]
        copies = start_all(pairs, sems)
        copies[0].wait()
        forward_b_ref[...] = dot(plain_ref[...], source_order(slot_ref, records, block, lambda i: i)).astype(BF)
        if n_sources == 1:
            forward_ref[...] = forward_b_ref[...]
        else:
            order = source_order(slot_ref, records, block, lambda i: partner(me, i // 4, i % 4, n, -1))
            forward_ref[...] = dot(plain_ref[...], order).astype(BF)
        for c in copies[1:]:
            c.wait()
        filter_gathers(arrived, layout, forward_ref, inverse_ref, response_ref, filtered_ref, per, block)
        mixed = filtered_ref.at[:, pl.ds((layout.tiles - 1) * LANES, LANES)]
        outs = start_all([(forward_b_ref, forward_b_hbm), (mixed, mixed_hbm)], sems, 4)
        out_ref[...] = dot(filtered_ref[...], table_ref[...])
        for c in outs + start_all([(out_ref, out_hbm)], sems, 6):
            c.wait()

    return kernel


def last_kernel(per, block, layout, n_traces, records):
    def kernel(arrived_hbm, forward_hbm, inverse_hbm, response_hbm, mixed_hbm, odd_table_hbm, even_hbm,
               out_hbm, arrived_ref, forward_ref, inverse_ref, response_ref, odd_table_ref, even_ref, filtered_ref, out_ref, sems):
        half = even_ref.shape[1]
        strip = STRIP
        cuts = [pl.ds(g * records, min(block, per - g) * records) for g in range(0, per, block)]
        mixed = filtered_ref.at[:, pl.ds(layout.tiles * LANES, LANES)]
        first = [(arrived_hbm, arrived_ref), (forward_hbm, forward_ref), (inverse_hbm, inverse_ref), (response_hbm, response_ref)]
        fetch = start_all(first + [(odd_table_hbm, odd_table_ref), (mixed_hbm, mixed)], sems)
        fetch += start_all([(even_hbm.at[c, :], even_ref.at[c, :]) for c in cuts], sems, len(fetch))
        for c in fetch[:4]:
            c.wait()
        arrived = [arrived_ref[s] for s in range(records)]
        row = lax.broadcasted_iota(jnp.int32, (UNIT, LANES), 0)
        lane = lax.broadcasted_iota(jnp.int32, (UNIT, LANES), 1)
        ends = sum(a[(layout.units - 1) * UNIT :].astype(F32) for a in arrived)
        ends = jnp.where((row == UNIT - 1) & (lane < 3), ends, 0.0)
        energy = jnp.sum(ends, keepdims=True)
        scale = lax.rsqrt(2.0 * FREQ * (energy * (1.0 / (n_traces * FREQ)) + energy_eps))
        copies = []
        for b in range(len(cuts)):
            filter_gathers(arrived, layout, forward_ref, inverse_ref, response_ref, filtered_ref, per, block, (b,))
            if b == 0:
                for c in fetch[4:6]:
                    c.wait()
            fetch[6 + b].wait()
            here = cuts[b]
            for s in range(0, half, strip):
                cols = slice(s, s + strip)
                odd = dot(filtered_ref[here, :], odd_table_ref[:, cols])
                even = even_ref[here, cols]
                out_ref[here, cols] = (even + odd) * scale
                out_ref[here, half + s : half + s + strip] = (even - odd) * scale
                pairs = []
                for there in (pl.ds(s, strip), pl.ds(half + s, strip)):
                    pairs.append((out_ref.at[here, there], out_hbm.at[here, there]))
                copies += start_all(pairs, sems, len(fetch) + len(copies))
        for c in copies:
            c.wait()

    return kernel


def shards(traces, cable_depth, receiver, shot_slot, gather_home):
    records = lax.axis_size("shard")
    n_rec = gather_home.shape[0]
    per = n_rec // records
    n_channels, n_samples = traces.shape
    half = n_samples // 2
    block = 2 * UNIT if records <= 16 else UNIT
    frame = -(-per // UNIT) * UNIT
    even_tiles, odd_tiles, mixed = bin_tiles()
    n_whole = len(even_tiles)
    layout = Layout(per, n_whole + 1, False)
    layout_b = Layout(per, n_whole, True)
    wave = wave_table(n_channels)
    even_table = time_table(n_samples, even_tiles + [mixed], 0)
    odd_table = time_table(n_samples, odd_tiles + [mixed], 1)
    mixed_odd = np.ascontiguousarray(odd_table[:, n_whole * LANES :])
    odd_whole = np.ascontiguousarray(odd_table[:, : n_whole * LANES])
    pad_bins = np.zeros((HALF,), np.int64)
    vertical = vertical_table(n_channels, n_samples, even_tiles + [mixed, pad_bins])
    vertical_b = vertical_table(n_channels, n_samples, odd_tiles)
    pairwise = records <= 16

    smem = pl.BlockSpec(memory_space=pltpu.SMEM)
    vmem = pl.BlockSpec(memory_space=pltpu.VMEM)
    hbm = pl.BlockSpec(memory_space=pltpu.HBM)
    alone = pltpu.CompilerParams(vmem_limit_bytes=ALL_VMEM)
    most = pltpu.CompilerParams(vmem_limit_bytes=MOST_VMEM)
    shared = pltpu.CompilerParams(vmem_limit_bytes=PART_VMEM)

    def scratch(array):
        return pltpu.VMEM(array.shape, array.dtype)

    n = records // 4
    planes = records // 2 if pairwise else 1
    *sources, odd, place, wave_kept, energy, odd_kept, vertical_kept = pl.pallas_call(
        front_kernel(per, frame, layout, records, planes),
        out_shape=(
            *(jax.ShapeDtypeStruct((records // planes, layout.units * UNIT, LANES), BF) for _ in range(planes)),
            pltpu.VMEM((n_channels, half), BF),
            pltpu.VMEM((records * frame, wave.shape[0]), BF),
            scratch(wave),
            pltpu.VMEM((1, LANES), F32),
            scratch(odd_whole),
            scratch(vertical_b),
        ),
        in_specs=[smem, vmem, vmem] + [hbm] * 7,
        out_specs=(vmem,) * (6 + planes),
        scratch_shapes=[
            scratch(vertical),
            scratch(traces),
            scratch(even_table),
            scratch(mixed_odd),
            pltpu.VMEM((n_channels, half), BF),
            pltpu.VMEM((records * frame, (n_whole + 1) * LANES), F32),
            pltpu.VMEM((2, n_whole + 1, wave.shape[0] // 2, LANES), F32),
            pltpu.SemaphoreType.DMA((10,)),
        ],
        compiler_params=pltpu.CompilerParams(vmem_limit_bytes=FRONT_VMEM),
        name="front",
    )(cable_depth, receiver, gather_home, vertical, wave, traces, even_table, mixed_odd, odd_whole, vertical_b)
    if pairwise:
        for chip in chips(records):
            route = [(s, partner(s, chip // 2, chip % 2 * 2, n, 1)) for s in range(records)]
            sources[chip] = lax.ppermute(sources[chip], "shard", route)
    else:
        sources = [lax.all_to_all(sources[0], "shard", split_axis=0, concat_axis=0, tiled=True)]

    second = pl.pallas_call(
        second_kernel(frame, layout_b, records),
        out_shape=jax.ShapeDtypeStruct((records, layout_b.units * UNIT, LANES), BF),
        in_specs=[smem] + [vmem] * 6,
        out_specs=vmem,
        scratch_shapes=[
            pltpu.VMEM((records * frame, n_whole * LANES), F32),
            pltpu.VMEM((2, n_whole, wave.shape[0] // 2, LANES), F32),
        ],
        compiler_params=shared,
        name="second",
    )
    message_b = second(cable_depth, energy, odd, place, wave_kept, odd_kept, vertical_kept)
    arrived_b = lax.all_to_all(message_b, "shard", split_axis=0, concat_axis=0, tiled=True)

    if pairwise:
        packed = pl.pallas_call(
            repack_kernel(planes),
            out_shape=jax.ShapeDtypeStruct((planes, *sources[0].shape[1:]), BF),
            in_specs=[vmem] * planes,
            out_specs=vmem,
            compiler_params=shared,
            name="repack",
        )(*sources)
        sources.append(lax.ppermute(packed, "shard", [(s, s ^ 1) for s in range(records)]))

    forward = shot_forward(records, block)
    inverse = shot_inverse(records)
    response = response_table(records, n_samples, even_tiles + [mixed])
    even_inverse = np.ascontiguousarray(even_table.T)
    even, forward_b, mixed_part = pl.pallas_call(
        even_kernel(per, block, layout, records, len(sources)),
        out_shape=(
            jax.ShapeDtypeStruct((per * records, half), F32),
            jax.ShapeDtypeStruct(forward.shape, BF),
            jax.ShapeDtypeStruct((per * records, LANES), BF),
        ),
        in_specs=[smem] + [hbm] * 4 + [vmem] * len(sources),
        out_specs=(hbm,) * 3,
        scratch_shapes=[
            pltpu.VMEM((per * records, half), F32),
            scratch(forward),
            scratch(forward),
            scratch(forward),
            scratch(inverse),
            scratch(response),
            scratch(even_inverse),
            pltpu.VMEM((per * records, (n_whole + 1) * LANES), BF),
            pltpu.SemaphoreType.DMA((7,)),
        ],
        compiler_params=shared,
        name="even",
    )(shot_slot, forward, inverse, response, even_inverse, *sources)
    out = pl.pallas_call(
        last_kernel(per, block, layout_b, n_channels * records, records),
        out_shape=jax.ShapeDtypeStruct((per * records, n_samples), F32),
        in_specs=[hbm] * 7,
        out_specs=hbm,
        scratch_shapes=[
            scratch(arrived_b),
            scratch(forward),
            scratch(inverse),
            pltpu.VMEM((2 * records, n_whole * LANES), F32),
            scratch(odd_table.T),
            pltpu.VMEM((per * records, half), F32),
            pltpu.VMEM((per * records, (n_whole + 1) * LANES), BF),
            pltpu.VMEM((per * records, n_samples), F32),
            pltpu.SemaphoreType.DMA((6 + -(-per // block) * (1 + 2 * (half // STRIP)),)),
        ],
        compiler_params=most,
        name="last",
    )(arrived_b, forward_b, inverse, response_table(records, n_samples, odd_tiles), mixed_part, np.ascontiguousarray(odd_table.T), even)
    return out.reshape(per, records, n_samples)


def solution(mesh):
    in_specs = (
        P(("groups", "shard"), None),
        P(("groups", "shard")),
        P(("groups", "shard")),
        P("groups"),
        P("groups"),
    )
    out_specs = P(("groups", "shard"), None, None)
    return jax.shard_map(shards, mesh=mesh, in_specs=in_specs, out_specs=out_specs, check_vma=False)
```

```python
import math

import jax
import jax.numpy as jnp
import ml_dtypes
import numpy as np
from jax import lax
from jax.experimental import pallas as pl
from jax.experimental.pallas import tpu as pltpu
from jax.sharding import PartitionSpec as P


FREQ = 576

sample_step = 0.002
water_speed = 1500.0
channel_spacing = 12.5
shot_spacing = 25.0
surface_reflect = 0.9
ghost_floor = 0.1
reject_speed = 1500.0
low_floor = 4.0 * math.pi
energy_eps = 1e-06

BF = jnp.bfloat16
F32 = jnp.float32
LANES = 128
HALF = 64
UNIT = 8
ALL_VMEM = 60 << 20
MOST_VMEM = 53 << 20
FRONT_VMEM = 52 << 20
PART_VMEM = 36 << 20


def to_bf16(table):
    return np.asarray(table, np.float32).astype(ml_dtypes.bfloat16)


def bin_tiles():
    odd = np.arange(1, FREQ, 2)
    fours = np.arange(0, FREQ, 4)
    twos = np.arange(2, FREQ, 4)
    whole = len(odd) // HALF
    left = len(odd) - whole * HALF
    half = len(fours) // HALF
    assert 2 * left == HALF and 2 * half == whole and len(fours) == len(twos)
    odd_tiles = [odd[left + j * HALF : left + (j + 1) * HALF] for j in range(whole)]
    even_tiles = [b[j * HALF : (j + 1) * HALF] for b in (fours, twos) for j in range(half)]
    mixed = np.concatenate([fours[half * HALF :], twos[half * HALF :], odd[:left]])
    return even_tiles, odd_tiles, mixed


def quarter_table(n_samples, tiles, mixed):
    full = time_table(n_samples, tiles + [mixed], 0)[: n_samples // 4].astype(np.float32)
    columns = len(tiles) * LANES
    parts = []
    for h in range(2):
        keep = np.tile(mixed % 4 == 2 * h, 2)[None, :]
        mine = full[:, h * columns // 2 : (h + 1) * columns // 2]
        parts.append(np.concatenate([mine, np.where(keep, full[:, columns:], 0.0)], axis=1).T)
    return to_bf16(np.stack(parts))


def time_table(n_samples, tiles, parity):
    samples = np.arange(n_samples // 2, dtype=np.int64)
    parts = []
    for bins in tiles:
        angle = (samples[:, None] * bins[None, :] % n_samples) * (2.0 * np.pi / n_samples)
        keep = (bins % 2 == parity).astype(np.float64)[None, :]
        parts += [np.cos(angle) * keep, -np.sin(angle) * keep]
    return to_bf16(np.concatenate(parts, axis=1))


def wave_rows(n_channels):
    return -(-(n_channels // 2 + 1) // 16) * 16


def wave_table(n_channels):
    rows = wave_rows(n_channels)
    k = np.arange(rows, dtype=np.int64)
    c = np.arange(n_channels, dtype=np.int64)
    angle = (k[:, None] * c[None, :] % n_channels) * (2.0 * np.pi / n_channels)
    live = (k <= n_channels // 2)[:, None]
    inner = ((k > 0) & (2 * k < n_channels))[:, None]
    return to_bf16(np.concatenate([np.cos(angle) * live, np.sin(angle) * inner], axis=0))


def vertical_table(n_channels, n_samples, tiles):
    rows = wave_rows(n_channels)
    k = np.minimum(np.arange(rows), n_channels // 2).astype(np.float64)
    kx = 2.0 * np.pi * k / (n_channels * channel_spacing)
    bins = np.concatenate(tiles).astype(np.float64)
    slow = 2.0 * np.pi * bins / (n_samples * sample_step) / water_speed
    return np.sqrt(np.maximum(slow[None, :] ** 2 - kx[:, None] ** 2, 0.0)).astype(np.float32)


def shot_basis(records):
    k = np.concatenate([np.arange(records + 1), np.arange(1, records)])
    p = np.arange(records)
    angle = (k[:, None] * p[None, :] % (2 * records)) * (np.pi / records)
    is_sin = (np.arange(2 * records) > records)[:, None]
    return np.where(is_sin, np.sin(angle), np.cos(angle)), k


def shot_forward(records, block):
    basis, _ = shot_basis(records)
    full = np.einsum("kp,gh->gkph", basis, np.eye(block))
    return to_bf16(full.reshape(block * 2 * records, records * block))


def shot_inverse(records):
    basis, _ = shot_basis(records)
    full = np.einsum("kp,gh->gphk", basis, np.eye(UNIT))
    return to_bf16(full.reshape(UNIT * records, UNIT * 2 * records))


def response_table(records, n_samples, tiles):
    _, k = shot_basis(records)
    single = (k == 0) | (k == records)
    parts = []
    for bins in tiles:
        angular = 2.0 * np.pi * bins.astype(np.float64) / (n_samples * sample_step)
        shot_number = 2.0 * np.pi * k / (2 * records * shot_spacing)
        ratio = reject_speed * shot_number[:, None] / (angular[None, :] + low_floor)
        value = 1.0 / (1.0 + ratio**4) / (2.0 * records)
        value = value * np.where(single, 1.0, 2.0)[:, None] * np.where(bins == 0, 1.0, 2.0)[None, :]
        parts += [value, value]
    return np.concatenate(parts, axis=1).astype(np.float32)


def sin_cos(angle):
    turns = jnp.floor(angle * (1.0 / math.pi) + 0.5)
    rest = ((angle - turns * 3.140625) - turns * 9.67502593994140625e-4) - turns * 1.509957990978376432e-7
    sq = rest * rest
    sine = -2.3889859e-8 * sq + 2.7525562e-6
    sine = sine * sq - 1.9840874e-4
    sine = sine * sq + 8.3333310e-3
    sine = sine * sq - 1.6666667e-1
    sine = sine * sq * rest + rest
    cosine = -2.605e-7 * sq + 2.47609e-5
    cosine = cosine * sq - 1.3888397e-3
    cosine = cosine * sq + 4.16666418e-2
    cosine = cosine * sq - 0.4999999963
    cosine = cosine * sq + 1.0
    return sine, cosine


def gains(vertical, depth, weight):
    sine, cosine = sin_cos(vertical * depth)
    double = 2.0 * sine
    less = sine * double
    top = 1.0 - surface_reflect
    bottom = 1.0 - 2.0 * surface_reflect + surface_reflect * surface_reflect + ghost_floor
    scale = weight / (bottom + 2.0 * surface_reflect * less)
    return (top + surface_reflect * less) * scale, (-surface_reflect * double) * cosine * scale


def tile_gains(gain_re, gain_im, second):
    lane = lax.broadcasted_iota(jnp.int32, gain_re.shape, 1)
    low = lane < HALF
    re_other = pltpu.roll(gain_re, HALF, 1)
    im_other = pltpu.roll(gain_im, HALF, 1)
    if second:
        return jnp.where(low, re_other, gain_re), jnp.where(low, -im_other, gain_im)
    return jnp.where(low, gain_re, re_other), jnp.where(low, -gain_im, im_other)


def dot(a, b):
    return jnp.dot(a, b, preferred_element_type=F32)


def lift(spec, factors_ref, first, wave_ref):
    rows = wave_ref.shape[0] // 2
    plain = dot(wave_ref[...], spec)
    lifted = []
    for t in range(spec.shape[1] // LANES):
        same = factors_ref[0, first + t]
        swapped = factors_ref[1, first + t]
        both = []
        for h in range(2):
            part = plain[h * rows : (h + 1) * rows, t * LANES : (t + 1) * LANES]
            both.append((part * same + pltpu.roll(part, HALF, 1) * swapped).astype(BF))
        lifted.append(jnp.concatenate(both, axis=0))
    return join(lifted)


def store_factors(factors_ref, vertical_ref, depth, n_channels, first=None):
    tiles = factors_ref.shape[1]
    row = lax.broadcasted_iota(jnp.int32, (vertical_ref.shape[0], LANES), 0)
    single = (row == 0) | (row * 2 == n_channels)
    weight = jnp.where(single, 1.0 / n_channels, 2.0 / n_channels)
    for t in range(0, tiles, 2) if first is None else (first,):
        gain_re, gain_im = gains(vertical_ref[:, t * HALF : (t + 2) * HALF], depth, weight)
        for h in range(min(2, tiles - t)):
            factors_ref[0, t + h], factors_ref[1, t + h] = tile_gains(gain_re, gain_im, h == 1)


def join(parts):
    return parts[0] if len(parts) == 1 else jnp.concatenate(parts, axis=1)


def energy_of(cleaned):
    total = jnp.sum(cleaned * cleaned, axis=0, keepdims=True)
    return sum(total[:, t * LANES : (t + 1) * LANES] for t in range(cleaned.shape[1] // LANES))


class Layout:
    def __init__(self, per, tiles):
        assert per >= 3
        self.whole = per // UNIT
        self.left = per % UNIT
        self.tiles = tiles
        self.shared = UNIT // self.left if self.left else 1
        self.left_units = -(-tiles // self.shared) if self.left else 0
        self.units = self.whole * tiles + self.left_units

    def unit(self, tile, u):
        if u < self.whole:
            return tile * self.whole + u, 0
        if u == self.whole and self.left:
            return self.whole * self.tiles + tile // self.shared, tile % self.shared * self.left
        return None, 0


def partner(me, dz, lo, n, sign):
    return (me // 4 + (dz if sign > 0 else n - dz)) % n * 4 + ((me % 4) ^ lo)


def chips(records):
    n = records // 4
    far = sorted(range(1, n), key=lambda d: min(d, n - d))
    return [2 * dz + dx for dz in far for dx in range(2)] + [1]


def place_message(placed, layout, frame, store, i, energy=None):
    mine = placed[i * frame : (i + 1) * frame]
    if energy is not None:
        top = jnp.concatenate([with_energy(mine[:UNIT, :LANES], energy), mine[:UNIT, LANES:]], axis=1)
        mine = top if frame == UNIT else jnp.concatenate([top, mine[UNIT:]], axis=0)
    parts = [mine[: layout.whole * UNIT, t * LANES : (t + 1) * LANES] for t in range(layout.tiles)] if layout.whole else []
    left = [jnp.zeros((UNIT, LANES), F32) for _ in range(layout.left_units)]
    if layout.left:
        row = lax.broadcasted_iota(jnp.int32, (UNIT, LANES), 0)
        for t in range(layout.tiles):
            unit = mine[layout.whole * UNIT : (layout.whole + 1) * UNIT, t * LANES : (t + 1) * LANES]
            shift = t % layout.shared * layout.left
            unit = jnp.where(row < layout.left, unit, 0.0)
            left[t // layout.shared] += pltpu.roll(unit, shift, 0) if shift else unit
    store(jnp.concatenate(parts + left, axis=0).astype(BF))


def split_energy(energy):
    total = jnp.sum(energy, axis=1, keepdims=True)
    high = total.astype(BF).astype(F32)
    middle = (total - high).astype(BF).astype(F32)
    return high, middle, total - high - middle


def with_energy(unit, pieces):
    row = lax.broadcasted_iota(jnp.int32, (UNIT, LANES), 0)
    lane = lax.broadcasted_iota(jnp.int32, (UNIT, LANES), 1)
    value = jnp.where(row == 0, pieces[0], jnp.where(row == 1, pieces[1], jnp.where(row == 2, pieces[2], 0.0)))
    return jnp.where(lane == HALF, value, unit)


def into(ref, index=None):
    def store(value):
        if index is None:
            ref[...] = value
        else:
            ref[index] = value

    return store


def start_all(pairs, sems, first=0):
    copies = [pltpu.make_async_copy(a, b, sems.at[first + i]) for i, (a, b) in enumerate(pairs)]
    for c in copies:
        c.start()
    return copies


def front_kernel(per, frame, layout, records, count):
    def kernel(depth_ref, receiver_ref, home_ref, vertical_hbm, wave_hbm, traces_hbm, table_hbm, mixed_hbm, *refs):
        later_hbm = refs[:2]
        *messages, sum_ref, place_ref, wave_ref, energy_ref = refs[2 : 6 + count]
        later = refs[6 + count : 8 + count]
        vertical_ref, traces_ref, table_ref, mixed_ref, odd_ref, placed_ref, factors_ref, sems = refs[8 + count :]
        me = lax.axis_index("shard")
        n_channels, n_samples = traces_ref.shape
        half = n_samples // 2
        steps = 3
        step = n_channels // steps
        pairs = [(traces_hbm.at[pl.ds(s * step, step), :], traces_ref.at[pl.ds(s * step, step), :]) for s in range(steps)]
        pairs = [(wave_hbm, wave_ref), *pairs, (table_hbm, table_ref), (mixed_hbm, mixed_ref), (vertical_hbm, vertical_ref)]
        copies = start_all(pairs, sems)
        n_rec = home_ref.shape[0]
        home = home_ref[...].reshape(1, n_rec)
        device = jnp.floor((home.astype(F32) + 0.5) * (1.0 / per)).astype(jnp.int32)
        n = records // 4
        turn = (device >> 2) - me // 4
        turn = jnp.where(turn < 0, turn + n, turn)
        home_row = (turn * 4 + ((device & 3) ^ (me % 4))) * frame + (home - device * per)
        both = jnp.concatenate([home_row >> 7, home_row & 127, jnp.zeros((14, n_rec), jnp.int32)], axis=0).astype(F32).astype(BF)
        to_bin = lax.broadcasted_iota(jnp.int32, (n_rec, n_channels), 0) == receiver_ref[...].reshape(1, n_channels)
        target = dot(both, jnp.where(to_bin, 1.0, 0.0).astype(BF))
        target = (target[0:1] * 128.0 + target[1:2]).astype(jnp.int32)
        picked = lax.broadcasted_iota(jnp.int32, (records * frame, n_channels), 0) == target
        picked = jnp.where(picked, 1.0, 0.0).astype(BF)
        copies[0].wait()
        place_ref[...] = lax.dot_general(picked, wave_ref[...], (((1,), (1,)), ((), ())), preferred_element_type=F32).astype(BF)
        outs = start_all(list(zip(later_hbm, later)), sems, len(copies))
        for s in range(steps):
            copies[1 + s].wait()
            part = pl.ds(s * step, step)
            first = traces_ref[part, :half]
            second = traces_ref[part, half:]
            sum_ref[part, :] = (first + second).astype(BF)
            odd_ref[part, :] = (first - second).astype(BF)
        for c in copies[-3:]:
            c.wait()
        spec = []
        for t in range(0, layout.tiles, 2):
            cols = slice(t * LANES, min(t + 2, layout.tiles) * LANES)
            got = dot(odd_ref[...], table_ref[:, cols])
            if t + 2 > layout.tiles:
                got = got + dot(sum_ref[...], mixed_ref[...])
            spec.append(got.astype(BF))
            store_factors(factors_ref, vertical_ref, depth_ref[0], n_channels, t)
        spec = jnp.concatenate(spec, axis=1)
        placed_ref[...] = dot(place_ref[...], lift(spec, factors_ref, 0, wave_ref))
        energy_ref[...] = energy_of(placed_ref[...])
        for i in range(records):
            store = into(messages[0], partner(me, i // 4, i % 4, n, 1)) if count == 1 else into(messages[i // 2], i % 2)
            place_message(placed_ref, layout, frame, store, i)
        for c in outs:
            c.wait()

    return kernel


def second_kernel(frame, layout, records):
    def kernel(depth_ref, energy_ref, sum_ref, place_ref, wave_ref, table_ref, vertical_ref, message_ref, placed_ref, factors_ref):
        me = lax.axis_index("shard")
        store_factors(factors_ref, vertical_ref, depth_ref[0], sum_ref.shape[0])
        spec = dot(sum_ref[...], table_ref[...]).astype(BF)
        placed_ref[...] = dot(place_ref[...], lift(spec, factors_ref, 0, wave_ref))
        pieces = split_energy(energy_ref[...] + energy_of(placed_ref[...]))
        for i in range(records):
            store = into(message_ref, partner(me, i // 4, i % 4, records // 4, 1))
            place_message(placed_ref, layout, frame, store, i, pieces)

    return kernel


def source_order(slot_ref, records, block, source):
    size = records * block
    column = lax.broadcasted_iota(jnp.int32, (1, size), 1)
    goal = jnp.zeros((1, size), jnp.int32)
    for i in range(records):
        goal = jnp.where(column // block == i, slot_ref[source(i)], goal)
    goal = goal * block + column % block
    return jnp.where(lax.broadcasted_iota(jnp.int32, (size, size), 0) == goal, 1.0, 0.0).astype(BF)


def filter_gathers(arrived, layout, forward_ref, inverse_ref, response_ref, out_ref, per, block, blocks=None):
    k = response_ref.shape[0]
    records = k // 2
    blank = jnp.zeros((UNIT, LANES), F32)
    units = [a.astype(F32) for a in arrived]
    for b in range(-(-per // block)) if blocks is None else blocks:
        live = min(block, per - b * block)
        sides = []
        for t in range(layout.tiles):
            pieces = []
            for a in units:
                for u in range(b * block // UNIT, (b + 1) * block // UNIT):
                    at, up = layout.unit(t, u)
                    piece = blank if at is None else a[at * UNIT : (at + 1) * UNIT]
                    pieces.append(pltpu.roll(piece, UNIT - up, 0) if up else piece)
            sides.append(jnp.concatenate(pieces, axis=0).astype(BF))
        part = dot(forward_ref[: live * k, :], join(sides)).reshape(live, k, layout.tiles * LANES)
        part = part * response_ref[...][None]
        part = part.reshape(live * k, layout.tiles * LANES).astype(BF)
        for g in range(0, live, UNIT):
            some = min(UNIT, live - g)
            back = dot(inverse_ref[: some * records, : some * k], part[g * k : (g + some) * k])
            row = (b * block + g) * records
            out_ref[row : row + some * records, : layout.tiles * LANES] = back.astype(BF)


def repack_kernel(n):
    def kernel(*refs):
        for chip in range(n):
            refs[n][chip] = refs[chip][1]

    return kernel


def odd_kernel(per, block, layout, records, n_sources):
    def kernel(slot_ref, forward_hbm, inverse_hbm, response_hbm, table_hbm, *refs):
        sources = refs[:n_sources]
        (out_hbm, forward_b_hbm, mixed_hbm, out_ref, forward_b_ref, forward_ref, plain_ref, inverse_ref, response_ref, table_ref,
         filtered_ref, sems) = refs[n_sources:]
        me = lax.axis_index("shard")
        n = records // 4
        arrived = []
        for i in range(records):
            if n_sources == 1:
                arrived.append(sources[0][i])
            elif i % 2:
                arrived.append(sources[-1][i // 2])
            else:
                arrived.append(sources[i // 2][0])
        pairs = [(forward_hbm, plain_ref), (inverse_hbm, inverse_ref), (response_hbm, response_ref), (table_hbm, table_ref)]
        copies = start_all(pairs, sems)
        copies[0].wait()
        forward_b_ref[...] = dot(plain_ref[...], source_order(slot_ref, records, block, lambda i: i)).astype(BF)
        if n_sources == 1:
            forward_ref[...] = forward_b_ref[...]
        else:
            order = source_order(slot_ref, records, block, lambda i: partner(me, i // 4, i % 4, n, -1))
            forward_ref[...] = dot(plain_ref[...], order).astype(BF)
        for c in copies[1:]:
            c.wait()
        filter_gathers(arrived, layout, forward_ref, inverse_ref, response_ref, filtered_ref, per, block)
        mixed = filtered_ref.at[:, pl.ds((layout.tiles - 1) * LANES, LANES)]
        outs = start_all([(forward_b_ref, forward_b_hbm), (mixed, mixed_hbm)], sems, 4)
        out_ref[...] = dot(filtered_ref[...], table_ref[...])
        for c in outs + start_all([(out_ref, out_hbm)], sems, 6):
            c.wait()

    return kernel


def last_kernel(per, block, layout, n_traces, records):
    def kernel(arrived_hbm, forward_hbm, inverse_hbm, response_hbm, mixed_hbm, table_hbm, odd_hbm,
               out_hbm, arrived_ref, forward_ref, inverse_ref, response_ref, table_ref, odd_ref, filtered_ref, out_ref, sems):
        quarter = odd_ref.shape[1] // 2
        cuts = [pl.ds(g * records, min(block, per - g) * records) for g in range(0, per, block)]
        mixed = filtered_ref.at[:, pl.ds(layout.tiles * LANES, LANES)]
        first = [(arrived_hbm, arrived_ref), (forward_hbm, forward_ref), (inverse_hbm, inverse_ref), (response_hbm, response_ref)]
        fetch = start_all(first + [(table_hbm, table_ref), (mixed_hbm, mixed)], sems)
        fetch += start_all([(odd_hbm.at[c, :], odd_ref.at[c, :]) for c in cuts], sems, len(fetch))
        for c in fetch[:4]:
            c.wait()
        arrived = [arrived_ref[s] for s in range(records)]
        row = lax.broadcasted_iota(jnp.int32, (UNIT, LANES), 0)
        lane = lax.broadcasted_iota(jnp.int32, (UNIT, LANES), 1)
        at = layout.unit(0, 0)[0] * UNIT
        ends = sum(a[at : at + UNIT].astype(F32) for a in arrived)
        energy = jnp.sum(jnp.where((row < 3) & (lane == HALF), ends, 0.0), keepdims=True)
        scale = lax.rsqrt(2.0 * FREQ * (energy * (1.0 / (n_traces * FREQ)) + energy_eps))
        whole = layout.tiles * LANES
        copies = []
        for b in range(len(cuts)):
            filter_gathers(arrived, layout, forward_ref, inverse_ref, response_ref, filtered_ref, per, block, (b,))
            if b == 0:
                for c in fetch[4:6]:
                    c.wait()
            fetch[6 + b].wait()
            here = cuts[b]
            left = filtered_ref[here, whole:]
            fours = dot(jnp.concatenate([filtered_ref[here, : whole // 2], left], axis=1), table_ref[0])
            twos = dot(jnp.concatenate([filtered_ref[here, whole // 2 : whole], left], axis=1), table_ref[1])
            for q, even in enumerate((fours + twos, fours - twos)):
                odd = odd_ref[here, q * quarter : (q + 1) * quarter]
                for p, value in enumerate((even + odd, even - odd)):
                    there = pl.ds((2 * p + q) * quarter, quarter)
                    out_ref[here, there] = value * scale
                    copies += start_all([(out_ref.at[here, there], out_hbm.at[here, there])], sems, len(fetch) + len(copies))
        for c in copies:
            c.wait()

    return kernel


def shards(traces, cable_depth, receiver, shot_slot, gather_home):
    records = lax.axis_size("shard")
    n_rec = gather_home.shape[0]
    per = n_rec // records
    n_channels, n_samples = traces.shape
    half = n_samples // 2
    block = 2 * UNIT if records <= 16 else UNIT
    frame = -(-per // UNIT) * UNIT
    even_tiles, odd_tiles, mixed = bin_tiles()
    n_whole = len(even_tiles)
    layout = Layout(per, n_whole + 1)
    layout_b = Layout(per, n_whole)
    wave = wave_table(n_channels)
    odd_table = time_table(n_samples, odd_tiles + [mixed], 1)
    even_whole = time_table(n_samples, even_tiles, 0)
    mixed_even = time_table(n_samples, [mixed], 0)
    back_table = quarter_table(n_samples, even_tiles, mixed)
    pad_bins = np.zeros((HALF,), np.int64)
    vertical = vertical_table(n_channels, n_samples, odd_tiles + [mixed, pad_bins])
    vertical_b = vertical_table(n_channels, n_samples, even_tiles)
    pairwise = records <= 16

    smem = pl.BlockSpec(memory_space=pltpu.SMEM)
    vmem = pl.BlockSpec(memory_space=pltpu.VMEM)
    hbm = pl.BlockSpec(memory_space=pltpu.HBM)
    alone = pltpu.CompilerParams(vmem_limit_bytes=ALL_VMEM)
    most = pltpu.CompilerParams(vmem_limit_bytes=MOST_VMEM)
    shared = pltpu.CompilerParams(vmem_limit_bytes=PART_VMEM)

    def scratch(array):
        return pltpu.VMEM(array.shape, array.dtype)

    n = records // 4
    planes = records // 2 if pairwise else 1
    made = pltpu.VMEM if pairwise else jax.ShapeDtypeStruct
    *sources, sums, place, wave_kept, energy, even_kept, vertical_kept = pl.pallas_call(
        front_kernel(per, frame, layout, records, planes),
        out_shape=(
            *(made((records // planes, layout.units * UNIT, LANES), BF) for _ in range(planes)),
            pltpu.VMEM((n_channels, half), BF),
            pltpu.VMEM((records * frame, wave.shape[0]), BF),
            scratch(wave),
            pltpu.VMEM((1, LANES), F32),
            scratch(even_whole),
            scratch(vertical_b),
        ),
        in_specs=[smem, vmem, vmem] + [hbm] * 7,
        out_specs=(vmem,) * (6 + planes),
        scratch_shapes=[
            scratch(vertical),
            scratch(traces),
            scratch(odd_table),
            scratch(mixed_even),
            pltpu.VMEM((n_channels, half), BF),
            pltpu.VMEM((records * frame, (n_whole + 1) * LANES), F32),
            pltpu.VMEM((2, n_whole + 1, wave.shape[0] // 2, LANES), F32),
            pltpu.SemaphoreType.DMA((10,)),
        ],
        compiler_params=pltpu.CompilerParams(vmem_limit_bytes=FRONT_VMEM),
        name="front",
    )(cable_depth, receiver, gather_home, vertical, wave, traces, odd_table, mixed_even, even_whole, vertical_b)
    if pairwise:
        for chip in chips(records):
            route = [(s, partner(s, chip // 2, chip % 2 * 2, n, 1)) for s in range(records)]
            sources[chip] = lax.ppermute(sources[chip], "shard", route)
    else:
        sources = [lax.all_to_all(sources[0], "shard", split_axis=0, concat_axis=0, tiled=True)]

    second = pl.pallas_call(
        second_kernel(frame, layout_b, records),
        out_shape=jax.ShapeDtypeStruct((records, layout_b.units * UNIT, LANES), BF),
        in_specs=[smem] + [vmem] * 6,
        out_specs=vmem,
        scratch_shapes=[
            pltpu.VMEM((records * frame, n_whole * LANES), F32),
            pltpu.VMEM((2, n_whole, wave.shape[0] // 2, LANES), F32),
        ],
        compiler_params=shared,
        name="second",
    )
    message_b = second(cable_depth, energy, sums, place, wave_kept, even_kept, vertical_kept)
    arrived_b = lax.all_to_all(message_b, "shard", split_axis=0, concat_axis=0, tiled=True)

    if pairwise:
        packed = pl.pallas_call(
            repack_kernel(planes),
            out_shape=jax.ShapeDtypeStruct((planes, *sources[0].shape[1:]), BF),
            in_specs=[vmem] * planes,
            out_specs=vmem,
            compiler_params=shared,
            name="repack",
        )(*sources)
        sources.append(lax.ppermute(packed, "shard", [(s, s ^ 1) for s in range(records)]))

    forward = shot_forward(records, block)
    inverse = shot_inverse(records)
    response = response_table(records, n_samples, odd_tiles + [mixed])
    odd_inverse = np.ascontiguousarray(odd_table.T)
    odd, forward_b, mixed_part = pl.pallas_call(
        odd_kernel(per, block, layout, records, len(sources)),
        out_shape=(
            jax.ShapeDtypeStruct((per * records, half), F32),
            jax.ShapeDtypeStruct(forward.shape, BF),
            jax.ShapeDtypeStruct((per * records, LANES), BF),
        ),
        in_specs=[smem] + [hbm] * 4 + [vmem] * len(sources),
        out_specs=(hbm,) * 3,
        scratch_shapes=[
            pltpu.VMEM((per * records, half), F32),
            scratch(forward),
            scratch(forward),
            scratch(forward),
            scratch(inverse),
            scratch(response),
            scratch(odd_inverse),
            pltpu.VMEM((per * records, (n_whole + 1) * LANES), BF),
            pltpu.SemaphoreType.DMA((7,)),
        ],
        compiler_params=shared,
        name="odd",
    )(shot_slot, forward, inverse, response, odd_inverse, *sources)
    out = pl.pallas_call(
        last_kernel(per, block, layout_b, n_channels * records, records),
        out_shape=jax.ShapeDtypeStruct((per * records, n_samples), F32),
        in_specs=[hbm] * 7,
        out_specs=hbm,
        scratch_shapes=[
            scratch(arrived_b),
            scratch(forward),
            scratch(inverse),
            pltpu.VMEM((2 * records, n_whole * LANES), F32),
            scratch(back_table),
            pltpu.VMEM((per * records, half), F32),
            pltpu.VMEM((per * records, (n_whole + 1) * LANES), BF),
            pltpu.VMEM((per * records, n_samples), F32),
            pltpu.SemaphoreType.DMA((6 + 5 * -(-per // block),)),
        ],
        compiler_params=most,
        name="last",
    )(arrived_b, forward_b, inverse, response_table(records, n_samples, even_tiles), mixed_part, back_table, odd)
    return out.reshape(per, records, n_samples)


def solution(mesh):
    in_specs = (
        P(("groups", "shard"), None),
        P(("groups", "shard")),
        P(("groups", "shard")),
        P("groups"),
        P("groups"),
    )
    out_specs = P(("groups", "shard"), None, None)
    return jax.shard_map(shards, mesh=mesh, in_specs=in_specs, out_specs=out_specs, check_vma=False)
```

```python
import math

import jax
import jax.numpy as jnp
import ml_dtypes
import numpy as np
from jax import lax
from jax.experimental import pallas as pl
from jax.experimental.pallas import tpu as pltpu
from jax.sharding import PartitionSpec as P


FREQ = 576

sample_step = 0.002
water_speed = 1500.0
channel_spacing = 12.5
shot_spacing = 25.0
surface_reflect = 0.9
ghost_floor = 0.1
reject_speed = 1500.0
low_floor = 4.0 * math.pi
energy_eps = 1e-06

BF = jnp.bfloat16
F32 = jnp.float32
LANES = 128
HALF = 64
UNIT = 8
ALL_VMEM = 60 << 20
MOST_VMEM = 53 << 20
FRONT_VMEM = 52 << 20
PART_VMEM = 36 << 20


def to_bf16(table):
    return np.asarray(table, np.float32).astype(ml_dtypes.bfloat16)


def bin_tiles():
    odd = np.arange(1, FREQ, 2)
    fours = np.arange(0, FREQ, 4)
    twos = np.arange(2, FREQ, 4)
    whole = len(odd) // HALF
    left = len(odd) - whole * HALF
    half = len(fours) // HALF
    assert 2 * left == HALF and 2 * half == whole and len(fours) == len(twos)
    odd_tiles = [odd[left + j * HALF : left + (j + 1) * HALF] for j in range(whole)]
    even_tiles = [b[j * HALF : (j + 1) * HALF] for b in (fours, twos) for j in range(half)]
    mixed = np.concatenate([fours[half * HALF :], twos[half * HALF :], odd[:left]])
    return even_tiles, odd_tiles, mixed


def quarter_table(n_samples, tiles, mixed):
    full = time_table(n_samples, tiles + [mixed], 0)[: n_samples // 4].astype(np.float32)
    columns = len(tiles) * LANES
    parts = []
    for h in range(2):
        keep = np.tile(mixed % 4 == 2 * h, 2)[None, :]
        mine = full[:, h * columns // 2 : (h + 1) * columns // 2]
        parts.append(np.concatenate([mine, np.where(keep, full[:, columns:], 0.0)], axis=1).T)
    return to_bf16(np.stack(parts))


def time_table(n_samples, tiles, parity):
    samples = np.arange(n_samples // 2, dtype=np.int64)
    parts = []
    for bins in tiles:
        angle = (samples[:, None] * bins[None, :] % n_samples) * (2.0 * np.pi / n_samples)
        keep = (bins % 2 == parity).astype(np.float64)[None, :]
        parts += [np.cos(angle) * keep, -np.sin(angle) * keep]
    return to_bf16(np.concatenate(parts, axis=1))


def wave_rows(n_channels):
    return -(-(n_channels // 2 + 1) // 16) * 16


def wave_table(n_channels):
    rows = wave_rows(n_channels)
    k = np.arange(rows, dtype=np.int64)
    c = np.arange(n_channels, dtype=np.int64)
    angle = (k[:, None] * c[None, :] % n_channels) * (2.0 * np.pi / n_channels)
    live = (k <= n_channels // 2)[:, None]
    inner = ((k > 0) & (2 * k < n_channels))[:, None]
    return to_bf16(np.concatenate([np.cos(angle) * live, np.sin(angle) * inner], axis=0))


def vertical_table(n_channels, n_samples, tiles):
    rows = wave_rows(n_channels)
    k = np.minimum(np.arange(rows), n_channels // 2).astype(np.float64)
    kx = 2.0 * np.pi * k / (n_channels * channel_spacing)
    bins = np.concatenate(tiles).astype(np.float64)
    slow = 2.0 * np.pi * bins / (n_samples * sample_step) / water_speed
    return np.sqrt(np.maximum(slow[None, :] ** 2 - kx[:, None] ** 2, 0.0)).astype(np.float32)


def shot_basis(records):
    k = np.concatenate([np.arange(records + 1), np.arange(1, records)])
    p = np.arange(records)
    angle = (k[:, None] * p[None, :] % (2 * records)) * (np.pi / records)
    is_sin = (np.arange(2 * records) > records)[:, None]
    return np.where(is_sin, np.sin(angle), np.cos(angle)), k


def shot_forward(records, block):
    basis, _ = shot_basis(records)
    full = np.einsum("kp,gh->gkph", basis, np.eye(block))
    return to_bf16(full.reshape(block * 2 * records, records * block))


def shot_inverse(records):
    basis, _ = shot_basis(records)
    full = np.einsum("kp,gh->gphk", basis, np.eye(UNIT))
    return to_bf16(full.reshape(UNIT * records, UNIT * 2 * records))


def response_table(records, n_samples, tiles):
    _, k = shot_basis(records)
    single = (k == 0) | (k == records)
    parts = []
    for bins in tiles:
        angular = 2.0 * np.pi * bins.astype(np.float64) / (n_samples * sample_step)
        shot_number = 2.0 * np.pi * k / (2 * records * shot_spacing)
        ratio = reject_speed * shot_number[:, None] / (angular[None, :] + low_floor)
        value = 1.0 / (1.0 + ratio**4) / (2.0 * records)
        value = value * np.where(single, 1.0, 2.0)[:, None] * np.where(bins == 0, 1.0, 2.0)[None, :]
        parts += [value, value]
    return np.concatenate(parts, axis=1).astype(np.float32)


def sin_cos(angle):
    turns = jnp.floor(angle * (1.0 / math.pi) + 0.5)
    rest = ((angle - turns * 3.140625) - turns * 9.67502593994140625e-4) - turns * 1.509957990978376432e-7
    sq = rest * rest
    sine = -2.3889859e-8 * sq + 2.7525562e-6
    sine = sine * sq - 1.9840874e-4
    sine = sine * sq + 8.3333310e-3
    sine = sine * sq - 1.6666667e-1
    sine = sine * sq * rest + rest
    cosine = -2.605e-7 * sq + 2.47609e-5
    cosine = cosine * sq - 1.3888397e-3
    cosine = cosine * sq + 4.16666418e-2
    cosine = cosine * sq - 0.4999999963
    cosine = cosine * sq + 1.0
    return sine, cosine


def gains(vertical, depth, weight):
    sine, cosine = sin_cos(vertical * depth)
    double = 2.0 * sine
    less = sine * double
    top = 1.0 - surface_reflect
    bottom = 1.0 - 2.0 * surface_reflect + surface_reflect * surface_reflect + ghost_floor
    scale = weight / (bottom + 2.0 * surface_reflect * less)
    return (top + surface_reflect * less) * scale, (-surface_reflect * double) * cosine * scale


def tile_gains(gain_re, gain_im, second):
    lane = lax.broadcasted_iota(jnp.int32, gain_re.shape, 1)
    low = lane < HALF
    re_other = pltpu.roll(gain_re, HALF, 1)
    im_other = pltpu.roll(gain_im, HALF, 1)
    if second:
        return jnp.where(low, re_other, gain_re), jnp.where(low, -im_other, gain_im)
    return jnp.where(low, gain_re, re_other), jnp.where(low, -gain_im, im_other)


def dot(a, b):
    return jnp.dot(a, b, preferred_element_type=F32)


def lift(spec, factors_ref, first, wave_ref):
    rows = wave_ref.shape[0] // 2
    plain = dot(wave_ref[...], spec)
    lifted = []
    for t in range(spec.shape[1] // LANES):
        same = factors_ref[0, first + t]
        swapped = factors_ref[1, first + t]
        both = []
        for h in range(2):
            part = plain[h * rows : (h + 1) * rows, t * LANES : (t + 1) * LANES]
            both.append((part * same + pltpu.roll(part, HALF, 1) * swapped).astype(BF))
        lifted.append(jnp.concatenate(both, axis=0))
    return join(lifted)


def store_factors(factors_ref, vertical_ref, depth, n_channels, first=None):
    tiles = factors_ref.shape[1]
    row = lax.broadcasted_iota(jnp.int32, (vertical_ref.shape[0], LANES), 0)
    single = (row == 0) | (row * 2 == n_channels)
    weight = jnp.where(single, 1.0 / n_channels, 2.0 / n_channels)
    for t in range(0, tiles, 2) if first is None else (first,):
        gain_re, gain_im = gains(vertical_ref[:, t * HALF : (t + 2) * HALF], depth, weight)
        for h in range(min(2, tiles - t)):
            factors_ref[0, t + h], factors_ref[1, t + h] = tile_gains(gain_re, gain_im, h == 1)


def join(parts):
    return parts[0] if len(parts) == 1 else jnp.concatenate(parts, axis=1)


def energy_of(cleaned):
    total = jnp.sum(cleaned * cleaned, axis=0, keepdims=True)
    return sum(total[:, t * LANES : (t + 1) * LANES] for t in range(cleaned.shape[1] // LANES))


class Layout:
    def __init__(self, per, tiles):
        assert per >= 3
        self.whole = per // UNIT
        self.left = per % UNIT
        self.tiles = tiles
        self.shared = UNIT // self.left if self.left else 1
        self.left_units = -(-tiles // self.shared) if self.left else 0
        self.units = self.whole * tiles + self.left_units
        self.packed = self.whole > 0 and self.left > 0 and UNIT % self.left == 0
        self.frame = self.whole * UNIT if self.packed else -(-per // UNIT) * UNIT

    def unit(self, tile, u):
        if u < self.whole:
            return tile * self.whole + u, 0
        if u == self.whole and self.left:
            return self.whole * self.tiles + tile // self.shared, tile % self.shared * self.left
        return None, 0


def partner(me, dz, lo, n, sign):
    return (me // 4 + (dz if sign > 0 else n - dz)) % n * 4 + ((me % 4) ^ lo)


def chips(records):
    n = records // 4
    far = sorted(range(1, n), key=lambda d: min(d, n - d))
    return [2 * dz + dx for dz in far for dx in range(2)] + [1]


def place_message(placed, layout, store, i, records, energy=None):
    frame = layout.frame
    mine = placed[i * frame : (i + 1) * frame]
    if energy is not None:
        top = jnp.concatenate([with_energy(mine[:UNIT, :LANES], energy), mine[:UNIT, LANES:]], axis=1)
        mine = top if frame == UNIT else jnp.concatenate([top, mine[UNIT:]], axis=0)
    parts = [mine[: layout.whole * UNIT, t * LANES : (t + 1) * LANES] for t in range(layout.tiles)] if layout.whole else []
    left = [jnp.zeros((UNIT, LANES), F32) for _ in range(layout.left_units)]
    if layout.left:
        row = lax.broadcasted_iota(jnp.int32, (UNIT, LANES), 0)
        if layout.packed:
            at = records * frame + i * layout.left // UNIT * UNIT
            last, off = placed[at : at + UNIT], i * layout.left % UNIT
        else:
            last, off = mine[layout.whole * UNIT : (layout.whole + 1) * UNIT], 0
        for t in range(layout.tiles):
            shift = t % layout.shared * layout.left
            unit = last[:, t * LANES : (t + 1) * LANES]
            move = (shift - off) % UNIT
            unit = pltpu.roll(unit, move, 0) if move else unit
            left[t // layout.shared] += jnp.where((row >= shift) & (row < shift + layout.left), unit, 0.0)
    store(jnp.concatenate(parts + left, axis=0).astype(BF))


def split_energy(energy):
    total = jnp.sum(energy, axis=1, keepdims=True)
    high = total.astype(BF).astype(F32)
    middle = (total - high).astype(BF).astype(F32)
    return high, middle, total - high - middle


def with_energy(unit, pieces):
    row = lax.broadcasted_iota(jnp.int32, (UNIT, LANES), 0)
    lane = lax.broadcasted_iota(jnp.int32, (UNIT, LANES), 1)
    value = jnp.where(row == 0, pieces[0], jnp.where(row == 1, pieces[1], jnp.where(row == 2, pieces[2], 0.0)))
    return jnp.where(lane == HALF, value, unit)


def into(ref, index=None):
    def store(value):
        if index is None:
            ref[...] = value
        else:
            ref[index] = value

    return store


def start_all(pairs, sems, first=0):
    copies = [pltpu.make_async_copy(a, b, sems.at[first + i]) for i, (a, b) in enumerate(pairs)]
    for c in copies:
        c.start()
    return copies


def front_kernel(per, rows, layout, records, count):
    def kernel(depth_ref, receiver_ref, home_ref, vertical_hbm, wave_hbm, traces_hbm, table_hbm, mixed_hbm, *refs):
        later_hbm = refs[:2]
        *messages, sum_ref, place_ref, wave_ref, energy_ref = refs[2 : 6 + count]
        later = refs[6 + count : 8 + count]
        vertical_ref, traces_ref, table_ref, mixed_ref, odd_ref, placed_ref, factors_ref, sems = refs[8 + count :]
        me = lax.axis_index("shard")
        n_channels, n_samples = traces_ref.shape
        half = n_samples // 2
        steps = 3
        step = n_channels // steps
        pairs = [(traces_hbm.at[pl.ds(s * step, step), :], traces_ref.at[pl.ds(s * step, step), :]) for s in range(steps)]
        pairs = [(wave_hbm, wave_ref), *pairs, (table_hbm, table_ref), (mixed_hbm, mixed_ref), (vertical_hbm, vertical_ref)]
        copies = start_all(pairs, sems)
        n_rec = home_ref.shape[0]
        home = home_ref[...].reshape(1, n_rec)
        device = jnp.floor((home.astype(F32) + 0.5) * (1.0 / per)).astype(jnp.int32)
        n = records // 4
        turn = (device >> 2) - me // 4
        turn = jnp.where(turn < 0, turn + n, turn)
        turn = turn * 4 + ((device & 3) ^ (me % 4))
        slot = home - device * per
        frame = layout.frame
        home_row = turn * frame + slot
        if layout.packed:
            home_row = jnp.where(slot < frame, home_row, records * frame + turn * layout.left + slot - frame)
        both = jnp.concatenate([home_row >> 7, home_row & 127, jnp.zeros((14, n_rec), jnp.int32)], axis=0).astype(F32).astype(BF)
        to_bin = lax.broadcasted_iota(jnp.int32, (n_rec, n_channels), 0) == receiver_ref[...].reshape(1, n_channels)
        target = dot(both, jnp.where(to_bin, 1.0, 0.0).astype(BF))
        target = (target[0:1] * 128.0 + target[1:2]).astype(jnp.int32)
        picked = lax.broadcasted_iota(jnp.int32, (rows, n_channels), 0) == target
        picked = jnp.where(picked, 1.0, 0.0).astype(BF)
        copies[0].wait()
        place_ref[...] = lax.dot_general(picked, wave_ref[...], (((1,), (1,)), ((), ())), preferred_element_type=F32).astype(BF)
        outs = start_all(list(zip(later_hbm, later)), sems, len(copies))
        for s in range(steps):
            copies[1 + s].wait()
            part = pl.ds(s * step, step)
            first = traces_ref[part, :half]
            second = traces_ref[part, half:]
            sum_ref[part, :] = (first + second).astype(BF)
            odd_ref[part, :] = (first - second).astype(BF)
        for c in copies[-3:]:
            c.wait()
        spec = []
        for t in range(0, layout.tiles, 2):
            cols = slice(t * LANES, min(t + 2, layout.tiles) * LANES)
            got = dot(odd_ref[...], table_ref[:, cols])
            if t + 2 > layout.tiles:
                got = got + dot(sum_ref[...], mixed_ref[...])
            spec.append(got.astype(BF))
            store_factors(factors_ref, vertical_ref, depth_ref[0], n_channels, t)
        spec = jnp.concatenate(spec, axis=1)
        placed_ref[...] = dot(place_ref[...], lift(spec, factors_ref, 0, wave_ref))
        energy_ref[...] = energy_of(placed_ref[...])
        for i in range(records):
            store = into(messages[0], partner(me, i // 4, i % 4, n, 1)) if count == 1 else into(messages[i // 2], i % 2)
            place_message(placed_ref, layout, store, i, records)
        for c in outs:
            c.wait()

    return kernel


def second_kernel(layout, records):
    def kernel(depth_ref, energy_ref, sum_ref, place_ref, wave_ref, table_ref, vertical_ref, message_ref, placed_ref, factors_ref):
        me = lax.axis_index("shard")
        store_factors(factors_ref, vertical_ref, depth_ref[0], sum_ref.shape[0])
        spec = dot(sum_ref[...], table_ref[...]).astype(BF)
        placed_ref[...] = dot(place_ref[...], lift(spec, factors_ref, 0, wave_ref))
        pieces = split_energy(energy_ref[...] + energy_of(placed_ref[...]))
        for i in range(records):
            store = into(message_ref, partner(me, i // 4, i % 4, records // 4, 1))
            place_message(placed_ref, layout, store, i, records, pieces)

    return kernel


def source_order(slot_ref, records, block, source):
    size = records * block
    column = lax.broadcasted_iota(jnp.int32, (1, size), 1)
    goal = jnp.zeros((1, size), jnp.int32)
    for i in range(records):
        goal = jnp.where(column // block == i, slot_ref[source(i)], goal)
    goal = goal * block + column % block
    return jnp.where(lax.broadcasted_iota(jnp.int32, (size, size), 0) == goal, 1.0, 0.0).astype(BF)


def filter_gathers(arrived, layout, forward_ref, inverse_ref, response_ref, out_ref, per, block, blocks=None):
    k = response_ref.shape[0]
    records = k // 2
    blank = jnp.zeros((UNIT, LANES), F32)
    units = [a.astype(F32) for a in arrived]
    for b in range(-(-per // block)) if blocks is None else blocks:
        live = min(block, per - b * block)
        sides = []
        for t in range(layout.tiles):
            pieces = []
            for a in units:
                for u in range(b * block // UNIT, (b + 1) * block // UNIT):
                    at, up = layout.unit(t, u)
                    piece = blank if at is None else a[at * UNIT : (at + 1) * UNIT]
                    pieces.append(pltpu.roll(piece, UNIT - up, 0) if up else piece)
            sides.append(jnp.concatenate(pieces, axis=0).astype(BF))
        part = dot(forward_ref[: live * k, :], join(sides)).reshape(live, k, layout.tiles * LANES)
        part = part * response_ref[...][None]
        part = part.reshape(live * k, layout.tiles * LANES).astype(BF)
        for g in range(0, live, UNIT):
            some = min(UNIT, live - g)
            back = dot(inverse_ref[: some * records, : some * k], part[g * k : (g + some) * k])
            row = (b * block + g) * records
            out_ref[row : row + some * records, : layout.tiles * LANES] = back.astype(BF)


def repack_kernel(n):
    def kernel(*refs):
        for chip in range(n):
            refs[n][chip] = refs[chip][1]

    return kernel


def odd_kernel(per, block, layout, records, n_sources):
    def kernel(slot_ref, forward_hbm, inverse_hbm, response_hbm, table_hbm, *refs):
        sources = refs[:n_sources]
        (out_hbm, forward_b_hbm, mixed_hbm, out_ref, forward_b_ref, forward_ref, plain_ref, inverse_ref, response_ref, table_ref,
         filtered_ref, sems) = refs[n_sources:]
        me = lax.axis_index("shard")
        n = records // 4
        arrived = []
        for i in range(records):
            if n_sources == 1:
                arrived.append(sources[0][i])
            elif i % 2:
                arrived.append(sources[-1][i // 2])
            else:
                arrived.append(sources[i // 2][0])
        pairs = [(forward_hbm, plain_ref), (inverse_hbm, inverse_ref), (response_hbm, response_ref), (table_hbm, table_ref)]
        copies = start_all(pairs, sems)
        copies[0].wait()
        forward_b_ref[...] = dot(plain_ref[...], source_order(slot_ref, records, block, lambda i: i)).astype(BF)
        if n_sources == 1:
            forward_ref[...] = forward_b_ref[...]
        else:
            order = source_order(slot_ref, records, block, lambda i: partner(me, i // 4, i % 4, n, -1))
            forward_ref[...] = dot(plain_ref[...], order).astype(BF)
        for c in copies[1:]:
            c.wait()
        filter_gathers(arrived, layout, forward_ref, inverse_ref, response_ref, filtered_ref, per, block)
        mixed = filtered_ref.at[:, pl.ds((layout.tiles - 1) * LANES, LANES)]
        outs = start_all([(forward_b_ref, forward_b_hbm), (mixed, mixed_hbm)], sems, 4)
        out_ref[...] = dot(filtered_ref[...], table_ref[...]).astype(BF)
        for c in outs + start_all([(out_ref, out_hbm)], sems, 6):
            c.wait()

    return kernel


def last_kernel(per, block, layout, n_traces, records):
    def kernel(arrived_hbm, forward_hbm, inverse_hbm, response_hbm, mixed_hbm, table_hbm, odd_hbm,
               out_hbm, arrived_ref, forward_ref, inverse_ref, response_ref, table_ref, odd_ref, filtered_ref, out_ref, sems):
        quarter = odd_ref.shape[1] // 2
        cuts = [pl.ds(g * records, min(block, per - g) * records) for g in range(0, per, block)]
        mixed = filtered_ref.at[:, pl.ds(layout.tiles * LANES, LANES)]
        first = [(arrived_hbm, arrived_ref), (forward_hbm, forward_ref), (inverse_hbm, inverse_ref), (response_hbm, response_ref)]
        fetch = start_all(first + [(table_hbm, table_ref), (mixed_hbm, mixed)], sems)
        fetch += start_all([(odd_hbm.at[c, :], odd_ref.at[c, :]) for c in cuts], sems, len(fetch))
        for c in fetch[:4]:
            c.wait()
        arrived = [arrived_ref[s] for s in range(records)]
        row = lax.broadcasted_iota(jnp.int32, (UNIT, LANES), 0)
        lane = lax.broadcasted_iota(jnp.int32, (UNIT, LANES), 1)
        at = layout.unit(0, 0)[0] * UNIT
        ends = sum(a[at : at + UNIT].astype(F32) for a in arrived)
        energy = jnp.sum(jnp.where((row < 3) & (lane == HALF), ends, 0.0), keepdims=True)
        scale = lax.rsqrt(2.0 * FREQ * (energy * (1.0 / (n_traces * FREQ)) + energy_eps))
        whole = layout.tiles * LANES
        copies = []
        for b in range(len(cuts)):
            filter_gathers(arrived, layout, forward_ref, inverse_ref, response_ref, filtered_ref, per, block, (b,))
            if b == 0:
                for c in fetch[4:6]:
                    c.wait()
            fetch[6 + b].wait()
            here = cuts[b]
            left = filtered_ref[here, whole:]
            fours = dot(jnp.concatenate([filtered_ref[here, : whole // 2], left], axis=1), table_ref[0])
            twos = dot(jnp.concatenate([filtered_ref[here, whole // 2 : whole], left], axis=1), table_ref[1])
            for q, even in enumerate((fours + twos, fours - twos)):
                odd = odd_ref[here, q * quarter : (q + 1) * quarter].astype(F32)
                for p, value in enumerate((even + odd, even - odd)):
                    there = pl.ds((2 * p + q) * quarter, quarter)
                    out_ref[here, there] = value * scale
                    copies += start_all([(out_ref.at[here, there], out_hbm.at[here, there])], sems, len(fetch) + len(copies))
        for c in copies:
            c.wait()

    return kernel


def shards(traces, cable_depth, receiver, shot_slot, gather_home):
    records = lax.axis_size("shard")
    n_rec = gather_home.shape[0]
    per = n_rec // records
    n_channels, n_samples = traces.shape
    half = n_samples // 2
    block = 2 * UNIT if records <= 16 else UNIT
    even_tiles, odd_tiles, mixed = bin_tiles()
    n_whole = len(even_tiles)
    layout = Layout(per, n_whole + 1)
    layout_b = Layout(per, n_whole)
    rows = records * (per if layout.packed else layout.frame)
    wave = wave_table(n_channels)
    odd_table = time_table(n_samples, odd_tiles + [mixed], 1)
    even_whole = time_table(n_samples, even_tiles, 0)
    mixed_even = time_table(n_samples, [mixed], 0)
    back_table = quarter_table(n_samples, even_tiles, mixed)
    pad_bins = np.zeros((HALF,), np.int64)
    vertical = vertical_table(n_channels, n_samples, odd_tiles + [mixed, pad_bins])
    vertical_b = vertical_table(n_channels, n_samples, even_tiles)
    pairwise = records <= 16

    smem = pl.BlockSpec(memory_space=pltpu.SMEM)
    vmem = pl.BlockSpec(memory_space=pltpu.VMEM)
    hbm = pl.BlockSpec(memory_space=pltpu.HBM)
    alone = pltpu.CompilerParams(vmem_limit_bytes=ALL_VMEM)
    most = pltpu.CompilerParams(vmem_limit_bytes=MOST_VMEM)
    shared = pltpu.CompilerParams(vmem_limit_bytes=PART_VMEM)

    def scratch(array):
        return pltpu.VMEM(array.shape, array.dtype)

    n = records // 4
    planes = records // 2 if pairwise else 1
    made = pltpu.VMEM if pairwise else jax.ShapeDtypeStruct
    *sources, sums, place, wave_kept, energy, even_kept, vertical_kept = pl.pallas_call(
        front_kernel(per, rows, layout, records, planes),
        out_shape=(
            *(made((records // planes, layout.units * UNIT, LANES), BF) for _ in range(planes)),
            pltpu.VMEM((n_channels, half), BF),
            pltpu.VMEM((rows, wave.shape[0]), BF),
            scratch(wave),
            pltpu.VMEM((1, LANES), F32),
            scratch(even_whole),
            scratch(vertical_b),
        ),
        in_specs=[smem, vmem, vmem] + [hbm] * 7,
        out_specs=(vmem,) * (6 + planes),
        scratch_shapes=[
            scratch(vertical),
            scratch(traces),
            scratch(odd_table),
            scratch(mixed_even),
            pltpu.VMEM((n_channels, half), BF),
            pltpu.VMEM((rows, (n_whole + 1) * LANES), F32),
            pltpu.VMEM((2, n_whole + 1, wave.shape[0] // 2, LANES), F32),
            pltpu.SemaphoreType.DMA((10,)),
        ],
        compiler_params=pltpu.CompilerParams(vmem_limit_bytes=FRONT_VMEM),
        name="front",
    )(cable_depth, receiver, gather_home, vertical, wave, traces, odd_table, mixed_even, even_whole, vertical_b)
    if pairwise:
        for chip in chips(records):
            route = [(s, partner(s, chip // 2, chip % 2 * 2, n, 1)) for s in range(records)]
            sources[chip] = lax.ppermute(sources[chip], "shard", route)
    else:
        sources = [lax.all_to_all(sources[0], "shard", split_axis=0, concat_axis=0, tiled=True)]

    second = pl.pallas_call(
        second_kernel(layout_b, records),
        out_shape=jax.ShapeDtypeStruct((records, layout_b.units * UNIT, LANES), BF),
        in_specs=[smem] + [vmem] * 6,
        out_specs=vmem,
        scratch_shapes=[
            pltpu.VMEM((rows, n_whole * LANES), F32),
            pltpu.VMEM((2, n_whole, wave.shape[0] // 2, LANES), F32),
        ],
        compiler_params=shared,
        name="second",
    )
    message_b = second(cable_depth, energy, sums, place, wave_kept, even_kept, vertical_kept)
    arrived_b = lax.all_to_all(message_b, "shard", split_axis=0, concat_axis=0, tiled=True)

    if pairwise:
        packed = pl.pallas_call(
            repack_kernel(planes),
            out_shape=jax.ShapeDtypeStruct((planes, *sources[0].shape[1:]), BF),
            in_specs=[vmem] * planes,
            out_specs=vmem,
            compiler_params=shared,
            name="repack",
        )(*sources)
        sources.append(lax.ppermute(packed, "shard", [(s, s ^ 1) for s in range(records)]))

    forward = shot_forward(records, block)
    inverse = shot_inverse(records)
    response = response_table(records, n_samples, odd_tiles + [mixed])
    odd_inverse = np.ascontiguousarray(odd_table.T)
    odd, forward_b, mixed_part = pl.pallas_call(
        odd_kernel(per, block, layout, records, len(sources)),
        out_shape=(
            jax.ShapeDtypeStruct((per * records, half), BF),
            jax.ShapeDtypeStruct(forward.shape, BF),
            jax.ShapeDtypeStruct((per * records, LANES), BF),
        ),
        in_specs=[smem] + [hbm] * 4 + [vmem] * len(sources),
        out_specs=(hbm,) * 3,
        scratch_shapes=[
            pltpu.VMEM((per * records, half), BF),
            scratch(forward),
            scratch(forward),
            scratch(forward),
            scratch(inverse),
            scratch(response),
            scratch(odd_inverse),
            pltpu.VMEM((per * records, (n_whole + 1) * LANES), BF),
            pltpu.SemaphoreType.DMA((7,)),
        ],
        compiler_params=shared,
        name="odd",
    )(shot_slot, forward, inverse, response, odd_inverse, *sources)
    out = pl.pallas_call(
        last_kernel(per, block, layout_b, n_channels * records, records),
        out_shape=jax.ShapeDtypeStruct((per * records, n_samples), F32),
        in_specs=[hbm] * 7,
        out_specs=hbm,
        scratch_shapes=[
            scratch(arrived_b),
            scratch(forward),
            scratch(inverse),
            pltpu.VMEM((2 * records, n_whole * LANES), F32),
            scratch(back_table),
            pltpu.VMEM((per * records, half), BF),
            pltpu.VMEM((per * records, (n_whole + 1) * LANES), BF),
            pltpu.VMEM((per * records, n_samples), F32),
            pltpu.SemaphoreType.DMA((6 + 5 * -(-per // block),)),
        ],
        compiler_params=most,
        name="last",
    )(arrived_b, forward_b, inverse, response_table(records, n_samples, even_tiles), mixed_part, back_table, odd)
    return out.reshape(per, records, n_samples)


def solution(mesh):
    in_specs = (
        P(("groups", "shard"), None),
        P(("groups", "shard")),
        P(("groups", "shard")),
        P("groups"),
        P("groups"),
    )
    out_specs = P(("groups", "shard"), None, None)
    return jax.shard_map(shards, mesh=mesh, in_specs=in_specs, out_specs=out_specs, check_vma=False)
```
